512 devices in a mesh: seq: 64 (over y, z), section: 8 (over x, core).
Axes of the slice: x: 4, y: 4, z: 16, core: 2. Of those that a mesh axis runs over, the one named last changes fastest.
Arguments:
- query_rows: bfloat16 [32768, 4096], P('seq', 'section'), may hold values from -6 to 6
- key_rows: bfloat16 [32768, 4096], P('seq', 'section'), may hold values from -6 to 6
- value_rows: bfloat16 [32768, 4096], P('seq', 'section'), may hold values from -6 to 6
- log_decay: float32 [32768, 32], P('seq', 'section'), may hold values from -1 to 0
- lengths: int32 [32], replicated, may hold values from 1 to 16384, as said below
- norm_gain: float32 [4096], P('section'), may hold values from 0.1 to 1.9
Outputs:
- next_input: bfloat16 [32768, 4096], P(('seq', 'section'))
The draws below stay inside these ranges and needn't reach their ends.
Inputs may be any that keep to these rules, and one draw needn't show every extreme that they name: The lengths of 32 documents in order, summing to 32768; the document at index (31) // 2 is the longest, exactly 16384 tokens, and starts at token 8192.
All inputs are finite; a program needn't handle non-finite values.
Results may differ from the reference program's by a relative error of at most 0.0058.
Values may be sent and summed in bfloat16 or wider, within the bound.
No kernel may reach another device: no remote copies, remote signals or barrier semaphores. Data moves between devices by JAX's collectives and lax.ppermute only.
A program may use at most 64 MiB of HBM per device.

```python
import math
import jax
import jax.numpy as jnp
from jax import lax

ATTENTION_PLANES = 32
DH = 128
TOK_DEV = 512
DOCS = 32
SEQUENCE_SYMBOLS = 32768


def split_span(key, total, pieces):
    if pieces == 1:
        return jnp.full((1,), total, jnp.int32)
    shuffled = jax.random.permutation(key, total - 1).astype(jnp.int32)
    cut_points = jnp.sort(shuffled[:pieces - 1]) + 1
    bounds = jnp.concatenate([jnp.zeros((1,), jnp.int32), cut_points.astype(jnp.int32), jnp.full((1,), total, jnp.int32)])
    return (bounds[1:] - bounds[:-1]).astype(jnp.int32)


def draw_lengths(key, part):
    half_length = SEQUENCE_SYMBOLS // 2
    quarter_length = SEQUENCE_SYMBOLS // 4
    before_docs = (DOCS - 1) // 2
    after_docs = DOCS - 1 - before_docs
    after_total = SEQUENCE_SYMBOLS - half_length - quarter_length
    before_lengths = split_span(jax.random.fold_in(key, 11), quarter_length, before_docs)
    after_lengths = split_span(jax.random.fold_in(key, 12), after_total, after_docs)
    return jnp.concatenate([before_lengths, jnp.full((1,), half_length, jnp.int32), after_lengths]).astype(jnp.int32)


def draw_log_decay(key, part):
    lookup_vector_matrix = jax.random.split(key, 7)
    blocks = SEQUENCE_SYMBOLS // TOK_DEV
    fast_share = 0.5
    fast_heads = jax.random.bernoulli(lookup_vector_matrix[0], fast_share, (1, ATTENTION_PLANES))
    fast_rate = 1.0 / jax.random.uniform(lookup_vector_matrix[1], (1, ATTENTION_PLANES), jnp.float32, 30.0, 50.0)
    slow_rate = math.log(10.0) / SEQUENCE_SYMBOLS * jax.random.uniform(lookup_vector_matrix[2], (1, ATTENTION_PLANES), jnp.float32, 0.1, 0.5)
    reference_fading_speed = jnp.where(fast_heads, fast_rate, slow_rate)
    segment_scaling_factor = jnp.exp(jax.random.uniform(lookup_vector_matrix[3], (blocks, ATTENTION_PLANES), jnp.float32, -math.log(2.0), math.log(2.0)))
    segment_scaling_factor = jnp.repeat(segment_scaling_factor, TOK_DEV, axis=0)
    rough_estimate_output = jax.random.uniform(lookup_vector_matrix[4], (SEQUENCE_SYMBOLS, ATTENTION_PLANES), jnp.float32, 0.5, 1.5)
    window_clusters = jax.random.bernoulli(lookup_vector_matrix[5], 2.0 / SEQUENCE_SYMBOLS, (SEQUENCE_SYMBOLS, ATTENTION_PLANES)).astype(jnp.float32)
    window_span = jax.random.uniform(lookup_vector_matrix[6], (SEQUENCE_SYMBOLS, ATTENTION_PLANES), jnp.float32, 0.22, 0.69)
    return -(reference_fading_speed * segment_scaling_factor * rough_estimate_output + window_clusters * window_span)


def shard_levels(stream_key, dims, cuts, least, largest):
    factor_of = 1.0
    for axis_at, blocks in cuts:
        draws = jax.random.uniform(jax.random.fold_in(jax.random.fold_in(stream_key, 6), axis_at), (blocks,), jnp.float32, least / len(cuts), largest / len(cuts))
        factor_of = factor_of * jnp.repeat(jnp.exp(draws), dims[axis_at] // blocks).reshape((-1,) + (1,) * (len(dims) - 1 - axis_at))
    return factor_of


def scatter_about(stream_key, extent, scale, bound, cuts=(), kind=jnp.bfloat16):
    drawn = scale * jax.random.normal(stream_key, extent, jnp.float32)
    if cuts:
        drawn = drawn * shard_levels(stream_key, extent, cuts, -0.22, 0.18)
    return jnp.clip(drawn, -bound, bound).astype(kind)


def setup_inputs(seed: int = 0) -> dict:
    arg_keys = jax.random.split(jax.random.key(seed), 7)
    return {
        "query_rows": scatter_about(arg_keys[0], (SEQUENCE_SYMBOLS, ATTENTION_PLANES * DH), 1.0, 6.0, ((0, 64), (1, 8))),
        "key_rows": scatter_about(arg_keys[1], (SEQUENCE_SYMBOLS, ATTENTION_PLANES * DH), 1.0, 6.0, ((0, 64), (1, 8))),
        "value_rows": scatter_about(arg_keys[2], (SEQUENCE_SYMBOLS, ATTENTION_PLANES * DH), 1.0, 6.0, ((0, 64), (1, 8))),
        "log_decay": draw_log_decay(jax.random.fold_in(arg_keys[6], 71), 0),
        "lengths": draw_lengths(jax.random.fold_in(arg_keys[6], 71), 0),
        "norm_gain": jnp.clip(1.0 + 0.18 * jax.random.normal(arg_keys[5], (ATTENTION_PLANES * DH,), jnp.float32), 0.1, 1.9),
    }


def block_terms(queries, key_block, value_block, decay_block, doc_ids, prev_doc):
    tok_rows = queries.shape[0]
    head_size = queries.shape[2]
    scale_factor = 1.0 / math.sqrt(head_size)
    cumulative = jnp.cumsum(decay_block, axis=0)
    position = jnp.arange(tok_rows, dtype=jnp.int32)
    allowed = (position[:, None] >= position[None, :]) & (doc_ids[:, None] == doc_ids[None, :])
    scores = jnp.einsum('thd,uhd->htu', queries.astype(jnp.float32), key_block.astype(jnp.float32))
    log_gap = cumulative.T[:, :, None] - cumulative.T[:, None, :]
    safe_gap = jnp.where(allowed[None], log_gap, 0.0)
    weights = jnp.where(allowed[None], scores * scale_factor * jnp.exp(safe_gap), 0.0).astype(jnp.bfloat16)
    within = jnp.einsum('htu,uhd->thd', weights.astype(jnp.float32), value_block.astype(jnp.float32))
    end_log = cumulative[-1]
    in_last = (doc_ids == doc_ids[-1]).astype(jnp.float32)
    key_scale = jnp.exp(end_log[None, :] - cumulative) * in_last[:, None]
    decayed_keys = (key_block.astype(jnp.float32) * key_scale[:, :, None]).astype(jnp.bfloat16)
    block_state = jnp.einsum('thd,the->hde', decayed_keys.astype(jnp.float32), value_block.astype(jnp.float32))
    opened = (doc_ids[-1] != prev_doc).astype(jnp.float32)
    decayed_queries = (queries.astype(jnp.float32) * (jnp.exp(cumulative) * scale_factor)[:, :, None]).astype(jnp.bfloat16)
    carried = (doc_ids == prev_doc).astype(jnp.float32)
    return (within, decayed_queries, carried, end_log, opened, block_state)

def finish(within, decayed_queries, carried, incoming, gain_heads):
    incoming_low = incoming.astype(jnp.bfloat16)
    carried_out = jnp.einsum('thd,hde->the', decayed_queries.astype(jnp.float32), incoming_low.astype(jnp.float32))
    attention = within + carried[:, None, None] * carried_out
    mean_square = lax.optimization_barrier(jnp.mean(attention * attention, axis=-1, keepdims=True))
    normed = attention * lax.rsqrt(mean_square + 1e-05) * gain_heads[None]
    return normed.astype(jnp.bfloat16)

def reference(query_rows, key_rows, value_rows, log_decay, lengths, norm_gain):
    blocks = SEQUENCE_SYMBOLS // TOK_DEV
    doc_ends = jnp.cumsum(lengths).astype(jnp.int32)
    positions = jnp.arange(SEQUENCE_SYMBOLS, dtype=jnp.int32)
    doc_ids = lax.optimization_barrier(jnp.sum((doc_ends[None, :] <= positions[:, None]).astype(jnp.int32), axis=1)).astype(jnp.int32)
    first_rows = jnp.arange(blocks, dtype=jnp.int32) * TOK_DEV
    prev_docs = lax.optimization_barrier(jnp.sum((doc_ends[None, :] <= (first_rows - 1)[:, None]).astype(jnp.int32), axis=1)).astype(jnp.int32)
    gain_heads = norm_gain.reshape(ATTENTION_PLANES, DH)
    inputs = (query_rows.reshape(blocks, TOK_DEV, ATTENTION_PLANES, DH), key_rows.reshape(blocks, TOK_DEV, ATTENTION_PLANES, DH), value_rows.reshape(blocks, TOK_DEV, ATTENTION_PLANES, DH), log_decay.reshape(blocks, TOK_DEV, ATTENTION_PLANES), doc_ids.reshape(blocks, TOK_DEV), prev_docs)

    def block_step(carry_state, items):
        queries, key_block, value_block, decay_block, block_docs, prev_doc = items
        within, decayed_queries, carried, end_log, opened, block_state = block_terms(queries, key_block, value_block, decay_block, block_docs, prev_doc)
        normed = finish(within, decayed_queries, carried, carry_state, gain_heads)
        new_state = block_state + ((1.0 - opened) * jnp.exp(end_log))[:, None, None] * carry_state
        return (new_state, normed)
    start_state = jnp.zeros((ATTENTION_PLANES, DH, DH), jnp.float32)
    last_state, outputs = lax.scan(block_step, start_state, inputs)
    return outputs.reshape(SEQUENCE_SYMBOLS, ATTENTION_PLANES * DH)
```

```python
import math

import jax
import jax.numpy as jnp
from jax import lax
from jax.experimental import pallas as pl
from jax.experimental.pallas import tpu as pltpu
from jax.sharding import PartitionSpec as P

F32, BF16 = jnp.float32, jnp.bfloat16
NEVER = -1e30
DECAY_ROWS = 8


def dot(a, b, contract):
    return lax.dot_general(a, b, ((contract[:1], contract[1:]), ((), ())), preferred_element_type=F32)


def three_parts(x):
    high = x.astype(BF16)
    rest = x - high.astype(F32)
    mid = rest.astype(BF16)
    return high, mid, (rest - mid.astype(F32)).astype(BF16)


def document_limits(lengths_ref, first_row, rows):
    last = first_row + rows - 1
    start_last, end_prev, begin = jnp.int32(0), jnp.int32(0), jnp.int32(0)
    found = jnp.bool_(False)
    for doc in range(lengths_ref.shape[0]):
        start_last = jnp.where(begin <= last, begin, start_last)
        end = begin + lengths_ref[doc]
        end_prev = jnp.where(found, end_prev, end)
        found = jnp.logical_or(found, end >= first_row)
        begin = end
    return start_last, end_prev


def state_kernel(lengths_ref, key_ref, value_ref, decay_ref, out_ref):
    rows, heads = decay_ref.shape
    dim = key_ref.shape[1] // heads
    holders, slots = out_ref.shape[0], heads * dim // out_ref.shape[0]
    first_row = lax.axis_index("seq") * rows
    start_last, _ = document_limits(lengths_ref, first_row, rows)
    row = lax.broadcasted_iota(jnp.int32, (rows, rows), 0)
    col = lax.broadcasted_iota(jnp.int32, (rows, rows), 1)
    later = (col > row).astype(F32).astype(BF16)
    decay = decay_ref[...]
    to_end = sum(dot(later, part, (1, 0)) for part in three_parts(decay))
    position = first_row + lax.broadcasted_iota(jnp.int32, (rows, 1), 0)
    in_last = position >= start_last
    key_scale = jnp.where(in_last, jnp.exp(to_end), 0.0)
    end_log = to_end[0:1, :] + decay[0:1, :]
    end_log = jnp.where(start_last >= first_row, NEVER, end_log)
    lines = lax.broadcasted_iota(jnp.int32, (DECAY_ROWS, dim), 0)
    per_head = holders // heads
    for head in range(heads):
        span = pl.ds(head * dim, dim)
        keys = (key_ref[:, span].astype(F32) * key_scale[:, head : head + 1]).astype(BF16)
        state = dot(keys, value_ref[:, span], (0, 0)).astype(BF16)
        high, mid, low = (p.astype(F32) for p in three_parts(end_log[:, head : head + 1]))
        sent = jnp.where(lines == 0, high, jnp.where(lines == 1, mid, jnp.where(lines == 2, low, 0.0)))
        sent = sent.astype(BF16)
        for i in range(per_head):
            out_ref[head * per_head + i, 0:slots, :] = state[i * slots : (i + 1) * slots, :]
            out_ref[head * per_head + i, slots : slots + DECAY_ROWS, :] = sent


def within_kernel(lengths_ref, query_ref, key_ref, value_ref, decay_ref, within_ref, decayed_ref):
    rows, heads = decay_ref.shape
    dim = key_ref.shape[1] // heads
    scale = 1.0 / math.sqrt(dim)
    step = 128
    first_row = lax.axis_index("seq") * rows
    _, end_prev = document_limits(lengths_ref, first_row, rows)
    row = lax.broadcasted_iota(jnp.int32, (rows, rows), 0)
    col = lax.broadcasted_iota(jnp.int32, (rows, rows), 1)
    upto = (col <= row).astype(F32).astype(BF16)
    parts = three_parts(decay_ref[...])
    cumul_col = sum(dot(upto, part, (1, 0)) for part in parts)
    cumul_row = sum(dot(part, upto, (0, 1)) for part in parts)
    spot_row = first_row + lax.broadcasted_iota(jnp.int32, (1, rows), 1)
    lane = lax.broadcasted_iota(jnp.int32, (1, dim), 1)
    doc_row = jnp.zeros((1, rows), F32)
    ends = jnp.zeros((1, dim), jnp.int32)
    end = jnp.int32(0)
    for doc in range(lengths_ref.shape[0]):
        end = end + lengths_ref[doc]
        doc_row = doc_row + jnp.where(spot_row >= end, 1.0, 0.0)
        ends = ends + jnp.where(lane >= doc, lengths_ref[doc], 0)
    position = first_row + lax.broadcasted_iota(jnp.int32, (rows, 1), 0)
    doc_col = jnp.sum(jnp.where(ends <= position, 1.0, 0.0), axis=1, keepdims=True)
    query_scale = jnp.where(position < end_prev, jnp.exp(cumul_col) * scale, 0.0)
    for head in range(heads):
        span = pl.ds(head * dim, dim)
        decayed_ref[:, span] = (query_ref[:, span].astype(F32) * query_scale[:, head : head + 1]).astype(BF16)
    for at in range(0, rows, step):
        upper = at + step
        t = at + lax.broadcasted_iota(jnp.int32, (step, upper), 0)
        u = lax.broadcasted_iota(jnp.int32, (step, upper), 1)
        allowed = jnp.logical_and(u <= t, doc_col[at:upper] == doc_row[:, :upper])
        shut = jnp.where(allowed, 0.0, NEVER)
        for head in range(heads):
            span = pl.ds(head * dim, dim)
            scores = dot(query_ref[pl.ds(at, step), span], key_ref[pl.ds(0, upper), span], (1, 1))
            gap = cumul_col[at:upper, head : head + 1] - cumul_row[head : head + 1, :upper]
            weights = jnp.where(allowed, scores * scale * jnp.exp(jnp.minimum(gap, 0.0) + shut), 0.0).astype(BF16)
            within_ref[pl.ds(at, step), span] = dot(weights, value_ref[pl.ds(0, upper), span], (1, 0))


def scan_kernel(taken_ref, out_ref):
    blocks, slots, dim = out_ref.shape
    carry = jnp.zeros((slots, dim), F32)
    for block in range(blocks):
        out_ref[block] = carry.astype(BF16)
        tail = taken_ref[block, slots : slots + DECAY_ROWS, :].astype(F32)
        kept = jnp.exp(tail[0:1] + tail[1:2] + tail[2:3])
        carry = taken_ref[block, 0:slots, :].astype(F32) + kept * carry


def finish_kernel(within_ref, decayed_ref, incoming_ref, gain_ref, out_ref):
    dim = incoming_ref.shape[1]
    for head in range(incoming_ref.shape[0] // dim):
        span = pl.ds(head * dim, dim)
        carried = dot(decayed_ref[:, span], incoming_ref[span, :], (1, 0))
        attention = within_ref[:, span] + carried
        mean_square = jnp.mean(attention * attention, axis=1, keepdims=True)
        out_ref[:, span] = (attention * lax.rsqrt(mean_square + 1e-05) * gain_ref[:, span]).astype(BF16)


def params():
    return pltpu.CompilerParams(vmem_limit_bytes=32 << 20)


def shards(query_rows, key_rows, value_rows, log_decay, lengths, norm_gain):
    rows, width = query_rows.shape
    heads = log_decay.shape[1]
    dim = width // heads
    blocks = lax.axis_size("seq")
    quarter = blocks // 4
    middle = list(range(quarter, 3 * quarter))
    chains = [middle, [b for b in range(blocks) if b not in middle]]
    holders = len(middle)
    slots = width // holders
    smem = pl.BlockSpec(memory_space=pltpu.SMEM)
    vmem = pl.BlockSpec(memory_space=pltpu.VMEM)

    states = pl.pallas_call(
        state_kernel,
        out_shape=jax.ShapeDtypeStruct((holders, slots + DECAY_ROWS, dim), BF16),
        in_specs=[smem, vmem, vmem, vmem],
        out_specs=vmem,
        compiler_params=params(),
        name="states",
    )(lengths, key_rows, value_rows, log_decay)
    taken = lax.all_to_all(states, "seq", split_axis=0, concat_axis=0, tiled=True, axis_index_groups=chains)
    within, decayed = pl.pallas_call(
        within_kernel,
        out_shape=(jax.ShapeDtypeStruct((rows, width), F32), jax.ShapeDtypeStruct((rows, width), BF16)),
        in_specs=[smem, vmem, vmem, vmem, vmem],
        out_specs=(vmem, vmem),
        compiler_params=params(),
        cost_estimate=pl.CostEstimate(
            flops=4 * rows * rows * width, bytes_accessed=9 * rows * width, transcendentals=rows * rows * heads
        ),
        name="within",
    )(lengths, query_rows, key_rows, value_rows, log_decay)
    given = pl.pallas_call(
        scan_kernel,
        out_shape=jax.ShapeDtypeStruct((holders, slots, dim), BF16),
        in_specs=[vmem],
        out_specs=vmem,
        compiler_params=params(),
        name="scan",
    )(taken)
    incoming = lax.all_to_all(given, "seq", split_axis=0, concat_axis=0, tiled=True, axis_index_groups=chains)
    step = rows // 4
    normed = pl.pallas_call(
        finish_kernel,
        out_shape=jax.ShapeDtypeStruct((rows, width), BF16),
        grid=(rows // step,),
        in_specs=[
            pl.BlockSpec((step, width), lambda i: (i, 0)),
            pl.BlockSpec((step, width), lambda i: (i, 0)),
            pl.BlockSpec((width, dim), lambda i: (0, 0)),
            pl.BlockSpec((1, width), lambda i: (0, 0)),
        ],
        out_specs=pl.BlockSpec((step, width), lambda i: (i, 0)),
        compiler_params=params(),
        name="finish",
    )(within, decayed, incoming.reshape(width, dim), norm_gain.reshape(1, width))
    return lax.all_to_all(normed, "section", split_axis=0, concat_axis=1, tiled=True)


def solution(mesh):
    placed = (
        P("seq", "section"),
        P("seq", "section"),
        P("seq", "section"),
        P("seq", "section"),
        P(),
        P("section"),
    )
    return jax.shard_map(
        shards, mesh=mesh, in_specs=placed, out_specs=P(("seq", "section"), None), check_vma=False
    )
```

```python
import math

import jax
import jax.numpy as jnp
from jax import lax
from jax.experimental import pallas as pl
from jax.experimental.pallas import tpu as pltpu
from jax.sharding import PartitionSpec as P

F32, BF16 = jnp.float32, jnp.bfloat16
NEVER = -1e30
DECAY_ROWS = 8


def dot(a, b, contract):
    return lax.dot_general(a, b, ((contract[:1], contract[1:]), ((), ())), preferred_element_type=F32)


def three_parts(x):
    high = x.astype(BF16)
    rest = x - high.astype(F32)
    mid = rest.astype(BF16)
    return high, mid, (rest - mid.astype(F32)).astype(BF16)


def document_limits(lengths_ref, first_row, rows):
    last = first_row + rows - 1
    start_last, end_prev, begin = jnp.int32(0), jnp.int32(0), jnp.int32(0)
    found = jnp.bool_(False)
    for doc in range(lengths_ref.shape[0]):
        start_last = jnp.where(begin <= last, begin, start_last)
        end = begin + lengths_ref[doc]
        end_prev = jnp.where(found, end_prev, end)
        found = jnp.logical_or(found, end >= first_row)
        begin = end
    return start_last, end_prev


def state_kernel(lengths_hbm, key_hbm, value_hbm, decay_hbm, out_ref, lengths_ref, keys_ref, values_ref, decay_ref, sems):
    heads, rows = decay_ref.shape
    dim = keys_ref.shape[1] // heads
    holders, slots = out_ref.shape[0], heads * dim // out_ref.shape[0]
    small = [
        pltpu.make_async_copy(lengths_hbm, lengths_ref, sems.at[2 * heads]),
        pltpu.make_async_copy(decay_hbm, decay_ref, sems.at[2 * heads + 1]),
    ]
    spans = [pl.ds(head * dim, dim) for head in range(heads)]
    large = []
    for head, span in enumerate(spans):
        large.append(pltpu.make_async_copy(key_hbm.at[:, span], keys_ref.at[:, span], sems.at[2 * head]))
        large.append(pltpu.make_async_copy(value_hbm.at[:, span], values_ref.at[:, span], sems.at[2 * head + 1]))
    for copy in small + large:
        copy.start()
    row = lax.broadcasted_iota(jnp.int32, (rows, rows), 0)
    col = lax.broadcasted_iota(jnp.int32, (rows, rows), 1)
    later = (col > row).astype(F32).astype(BF16)
    for copy in small:
        copy.wait()
    first_row = lax.axis_index("seq") * rows
    start_last, _ = document_limits(lengths_ref, first_row, rows)
    parts = three_parts(decay_ref[...])
    to_end = sum(dot(later, part, (1, 1)) for part in parts)
    all_log = sum(dot(jnp.ones((8, rows), BF16), part, (1, 1)) for part in parts)
    position = first_row + lax.broadcasted_iota(jnp.int32, (rows, 1), 0)
    key_scale = jnp.where(position >= start_last, jnp.exp(to_end), 0.0)
    end_log = jnp.where(start_last >= first_row, NEVER, all_log[0:1, :])
    lines = lax.broadcasted_iota(jnp.int32, (DECAY_ROWS, dim), 0)
    per_head = holders // heads
    for head, span in enumerate(spans):
        high, mid, low = (p.astype(F32) for p in three_parts(end_log[:, head : head + 1]))
        sent = jnp.where(lines == 0, high, jnp.where(lines == 1, mid, jnp.where(lines == 2, low, 0.0)))
        sent = sent.astype(BF16)
        large[2 * head].wait()
        keys = (keys_ref[:, span].astype(F32) * key_scale[:, head : head + 1]).astype(BF16)
        large[2 * head + 1].wait()
        state = dot(keys, values_ref[:, span], (0, 0)).astype(BF16)
        for i in range(per_head):
            out_ref[head * per_head + i, 0:slots, :] = state[i * slots : (i + 1) * slots, :]
            out_ref[head * per_head + i, slots : slots + DECAY_ROWS, :] = sent


def within_kernel(lengths_ref, query_ref, key_ref, value_ref, decay_ref, gain_ref, within_ref, decayed_ref, staged_ref):
    heads, rows = decay_ref.shape
    staged_ref[...] = gain_ref[...]
    dim = key_ref.shape[1] // heads
    scale = 1.0 / math.sqrt(dim)
    step = 128
    first_row = lax.axis_index("seq") * rows
    _, end_prev = document_limits(lengths_ref, first_row, rows)
    row = lax.broadcasted_iota(jnp.int32, (rows, rows), 0)
    col = lax.broadcasted_iota(jnp.int32, (rows, rows), 1)
    upto = (col <= row).astype(F32).astype(BF16)
    parts = three_parts(decay_ref[...])
    cumul_col = sum(dot(upto, part, (1, 1)) for part in parts)
    cumul_row = sum(dot(part, upto, (1, 1)) for part in parts)
    spot_row = first_row + lax.broadcasted_iota(jnp.int32, (1, rows), 1)
    lane = lax.broadcasted_iota(jnp.int32, (1, dim), 1)
    doc_row = jnp.zeros((1, rows), F32)
    ends = jnp.zeros((1, dim), jnp.int32)
    end = jnp.int32(0)
    for doc in range(lengths_ref.shape[0]):
        end = end + lengths_ref[doc]
        doc_row = doc_row + jnp.where(spot_row >= end, 1.0, 0.0)
        ends = ends + jnp.where(lane >= doc, lengths_ref[doc], 0)
    position = first_row + lax.broadcasted_iota(jnp.int32, (rows, 1), 0)
    doc_col = jnp.sum(jnp.where(ends <= position, 1.0, 0.0), axis=1, keepdims=True)
    query_scale = jnp.where(position < end_prev, jnp.exp(cumul_col) * scale, 0.0)
    for head in range(heads):
        span = pl.ds(head * dim, dim)
        decayed_ref[:, span] = (query_ref[:, span].astype(F32) * query_scale[:, head : head + 1]).astype(BF16)
    for at in range(0, rows, step):
        upper = at + step
        t = at + lax.broadcasted_iota(jnp.int32, (step, upper), 0)
        u = lax.broadcasted_iota(jnp.int32, (step, upper), 1)
        allowed = jnp.logical_and(u <= t, doc_col[at:upper] == doc_row[:, :upper])
        shut = jnp.where(allowed, 0.0, NEVER)
        for head in range(heads):
            span = pl.ds(head * dim, dim)
            scores = dot(query_ref[pl.ds(at, step), span], key_ref[pl.ds(0, upper), span], (1, 1))
            gap = cumul_col[at:upper, head : head + 1] - cumul_row[head : head + 1, :upper]
            weights = jnp.where(allowed, scores * scale * jnp.exp(jnp.minimum(gap, 0.0) + shut), 0.0).astype(BF16)
            within_ref[pl.ds(at, step), span] = dot(weights, value_ref[pl.ds(0, upper), span], (1, 0))


def scan_kernel(taken_ref, out_ref):
    blocks, slots, dim = out_ref.shape
    carry = jnp.zeros((slots, dim), F32)
    for block in range(blocks):
        out_ref[block] = carry.astype(BF16)
        tail = taken_ref[block, slots : slots + DECAY_ROWS, :].astype(F32)
        kept = jnp.exp(tail[0:1] + tail[1:2] + tail[2:3])
        carry = taken_ref[block, 0:slots, :].astype(F32) + kept * carry


def finish_kernel(within_ref, decayed_ref, incoming_ref, gain_ref, out_ref):
    dim = incoming_ref.shape[1]
    for head in range(incoming_ref.shape[0] // dim):
        span = pl.ds(head * dim, dim)
        carried = dot(decayed_ref[:, span], incoming_ref[span, :], (1, 0))
        attention = within_ref[:, span] + carried
        mean_square = jnp.mean(attention * attention, axis=1, keepdims=True)
        out_ref[:, span] = (attention * lax.rsqrt(mean_square + 1e-05) * gain_ref[:, span]).astype(BF16)


def params(mib=32):
    return pltpu.CompilerParams(vmem_limit_bytes=mib << 20)


def shards(query_rows, key_rows, value_rows, log_decay, lengths, norm_gain):
    rows, width = query_rows.shape
    heads = log_decay.shape[1]
    dim = width // heads
    blocks = lax.axis_size("seq")
    quarter = blocks // 4
    middle = list(range(quarter, 3 * quarter))
    chains = [middle, [b for b in range(blocks) if b not in middle]]
    holders = len(middle)
    slots = width // holders
    decay_rows = log_decay.T
    hbm = pl.BlockSpec(memory_space=pltpu.HBM)
    smem = pl.BlockSpec(memory_space=pltpu.SMEM)
    vmem = pl.BlockSpec(memory_space=pltpu.VMEM)

    states = pl.pallas_call(
        state_kernel,
        out_shape=jax.ShapeDtypeStruct((holders, slots + DECAY_ROWS, dim), BF16),
        in_specs=[hbm, hbm, hbm, hbm],
        out_specs=vmem,
        scratch_shapes=[
            pltpu.SMEM(lengths.shape, lengths.dtype),
            pltpu.VMEM((rows, width), BF16),
            pltpu.VMEM((rows, width), BF16),
            pltpu.VMEM((heads, rows), F32),
            pltpu.SemaphoreType.DMA((2 * heads + 2,)),
        ],
        compiler_params=params(60),
        name="states",
    )(lengths, key_rows, value_rows, decay_rows)
    taken = lax.all_to_all(states, "seq", split_axis=0, concat_axis=0, tiled=True, axis_index_groups=chains)
    within, decayed, gain = pl.pallas_call(
        within_kernel,
        out_shape=(
            jax.ShapeDtypeStruct((rows, width), F32),
            jax.ShapeDtypeStruct((rows, width), BF16),
            jax.ShapeDtypeStruct((1, width), F32),
        ),
        in_specs=[smem, vmem, vmem, vmem, vmem, vmem],
        out_specs=(vmem, vmem, vmem),
        compiler_params=params(),
        cost_estimate=pl.CostEstimate(
            flops=4 * rows * rows * width, bytes_accessed=9 * rows * width, transcendentals=rows * rows * heads
        ),
        name="within",
    )(lengths, query_rows, key_rows, value_rows, decay_rows, norm_gain.reshape(1, width))
    given = pl.pallas_call(
        scan_kernel,
        out_shape=jax.ShapeDtypeStruct((holders, slots, dim), BF16),
        in_specs=[vmem],
        out_specs=vmem,
        compiler_params=params(),
        name="scan",
    )(taken)
    incoming = lax.all_to_all(given, "seq", split_axis=0, concat_axis=0, tiled=True, axis_index_groups=chains)
    normed = pl.pallas_call(
        finish_kernel,
        out_shape=jax.ShapeDtypeStruct((rows, width), BF16),
        in_specs=[vmem] * 4,
        out_specs=vmem,
        compiler_params=params(),
        name="finish",
    )(within, decayed, incoming.reshape(width, dim), gain)
    return lax.all_to_all(normed, "section", split_axis=0, concat_axis=1, tiled=True)


def solution(mesh):
    placed = (
        P("seq", "section"),
        P("seq", "section"),
        P("seq", "section"),
        P("seq", "section"),
        P(),
        P("section"),
    )
    return jax.shard_map(
        shards, mesh=mesh, in_specs=placed, out_specs=P(("seq", "section"), None), check_vma=False
    )
```

```python
import math

import jax
import jax.numpy as jnp
from jax import lax
from jax.experimental import pallas as pl
from jax.experimental.pallas import tpu as pltpu
from jax.sharding import PartitionSpec as P

F32, BF16 = jnp.float32, jnp.bfloat16
NEVER = -1e30
PAIR = 2


def dot(a, b, contract):
    return lax.dot_general(a, b, ((contract[:1], contract[1:]), ((), ())), preferred_element_type=F32)


def three_parts(x):
    high = x.astype(BF16)
    rest = x - high.astype(F32)
    mid = rest.astype(BF16)
    return high, mid, (rest - mid.astype(F32)).astype(BF16)


def document_limits(lengths_ref, first_row, rows):
    last = first_row + rows - 1
    start_last, end_prev, begin = jnp.int32(0), jnp.int32(0), jnp.int32(0)
    found = jnp.bool_(False)
    for doc in range(lengths_ref.shape[0]):
        start_last = jnp.where(begin <= last, begin, start_last)
        end = begin + lengths_ref[doc]
        end_prev = jnp.where(found, end_prev, end)
        found = jnp.logical_or(found, end >= first_row)
        begin = end
    return start_last, end_prev


def state_kernel(lengths_hbm, key_hbm, value_hbm, decay_hbm, out_ref, lengths_ref, keys_ref, values_ref, decay_ref, sems):
    heads, rows = decay_ref.shape
    dim = keys_ref.shape[1] // heads
    holders, slots = out_ref.shape[0], heads * dim // out_ref.shape[0]
    small = [
        pltpu.make_async_copy(lengths_hbm, lengths_ref, sems.at[2 * heads]),
        pltpu.make_async_copy(decay_hbm, decay_ref, sems.at[2 * heads + 1]),
    ]
    spans = [pl.ds(head * dim, dim) for head in range(heads)]
    large = []
    for head, span in enumerate(spans):
        large.append(pltpu.make_async_copy(key_hbm.at[:, span], keys_ref.at[:, span], sems.at[2 * head]))
        large.append(pltpu.make_async_copy(value_hbm.at[:, span], values_ref.at[:, span], sems.at[2 * head + 1]))
    for copy in small + large:
        copy.start()
    row = lax.broadcasted_iota(jnp.int32, (rows, rows), 0)
    col = lax.broadcasted_iota(jnp.int32, (rows, rows), 1)
    later = (col > row).astype(F32).astype(BF16)
    for copy in small:
        copy.wait()
    first_row = lax.axis_index("seq") * rows
    start_last, _ = document_limits(lengths_ref, first_row, rows)
    parts = three_parts(decay_ref[...])
    to_end = sum(dot(later, part, (1, 1)) for part in parts)
    all_log = sum(dot(jnp.ones((8, rows), BF16), part, (1, 1)) for part in parts)
    position = first_row + lax.broadcasted_iota(jnp.int32, (rows, 1), 0)
    key_scale = jnp.where(position >= start_last, jnp.exp(to_end), 0.0)
    end_log = jnp.where(start_last >= first_row, NEVER, all_log[0:1, :])
    lane = lax.broadcasted_iota(jnp.int32, (PAIR, dim), 1)
    per_head = holders // heads
    for head, span in enumerate(spans):
        high, mid, low = (p.astype(F32) for p in three_parts(end_log[:, head : head + 1]))
        sent = jnp.where(lane == 0, high, jnp.where(lane == 1, mid, jnp.where(lane == 2, low, 0.0)))
        sent = sent.astype(BF16)
        large[2 * head].wait()
        keys = (keys_ref[:, span].astype(F32) * key_scale[:, head : head + 1]).astype(BF16)
        large[2 * head + 1].wait()
        state = dot(keys, values_ref[:, span], (0, 0)).astype(BF16)
        for i in range(per_head):
            for pair in range(slots // PAIR):
                at = i * slots + pair * PAIR
                out_ref[head * per_head + i, pair] = state[at : at + PAIR, :]
            out_ref[head * per_head + i, slots // PAIR] = sent


def within_kernel(lengths_ref, query_ref, key_ref, value_ref, decay_ref, gain_ref, within_ref, decayed_ref, staged_ref):
    heads, rows = decay_ref.shape
    staged_ref[...] = gain_ref[...]
    dim = key_ref.shape[1] // heads
    scale = 1.0 / math.sqrt(dim)
    step = 128
    first_row = lax.axis_index("seq") * rows
    _, end_prev = document_limits(lengths_ref, first_row, rows)
    row = lax.broadcasted_iota(jnp.int32, (rows, rows), 0)
    col = lax.broadcasted_iota(jnp.int32, (rows, rows), 1)
    upto = (col <= row).astype(F32).astype(BF16)
    parts = three_parts(decay_ref[...])
    cumul_col = sum(dot(upto, part, (1, 1)) for part in parts)
    cumul_row = sum(dot(part, upto, (1, 1)) for part in parts)
    spot_row = first_row + lax.broadcasted_iota(jnp.int32, (1, rows), 1)
    lane = lax.broadcasted_iota(jnp.int32, (1, dim), 1)
    doc_row = jnp.zeros((1, rows), F32)
    ends = jnp.zeros((1, dim), jnp.int32)
    end = jnp.int32(0)
    for doc in range(lengths_ref.shape[0]):
        end = end + lengths_ref[doc]
        doc_row = doc_row + jnp.where(spot_row >= end, 1.0, 0.0)
        ends = ends + jnp.where(lane >= doc, lengths_ref[doc], 0)
    position = first_row + lax.broadcasted_iota(jnp.int32, (rows, 1), 0)
    doc_col = jnp.sum(jnp.where(ends <= position, 1.0, 0.0), axis=1, keepdims=True)
    query_scale = jnp.where(position < end_prev, jnp.exp(cumul_col) * scale, 0.0)
    for head in range(heads):
        span = pl.ds(head * dim, dim)
        decayed_ref[:, span] = (query_ref[:, span].astype(F32) * query_scale[:, head : head + 1]).astype(BF16)
    for at in range(0, rows, step):
        upper = at + step
        t = at + lax.broadcasted_iota(jnp.int32, (step, upper), 0)
        u = lax.broadcasted_iota(jnp.int32, (step, upper), 1)
        allowed = jnp.logical_and(u <= t, doc_col[at:upper] == doc_row[:, :upper])
        shut = jnp.where(allowed, 0.0, NEVER)
        for head in range(heads):
            span = pl.ds(head * dim, dim)
            scores = dot(query_ref[pl.ds(at, step), span], key_ref[pl.ds(0, upper), span], (1, 1))
            gap = cumul_col[at:upper, head : head + 1] - cumul_row[head : head + 1, :upper]
            weights = jnp.where(allowed, scores * scale * jnp.exp(jnp.minimum(gap, 0.0) + shut), 0.0).astype(BF16)
            within_ref[pl.ds(at, step), span] = dot(weights, value_ref[pl.ds(0, upper), span], (1, 0))


def kept_of(taken_ref, block):
    parts = taken_ref[block, taken_ref.shape[1] - 1].astype(F32)[0:1, 0:3]
    return jnp.exp(jnp.sum(parts, axis=1, keepdims=True))


def total_kernel(taken_ref, total_ref):
    blocks, pairs = taken_ref.shape[0], taken_ref.shape[1] - 1
    carry = jnp.zeros(total_ref.shape, F32)
    for block in range(blocks):
        carry = taken_ref[block, 0:pairs].astype(F32) + kept_of(taken_ref, block) * carry
    total_ref[...] = carry


def scan_kernel(taken_ref, entering_ref, out_ref):
    blocks, pairs = taken_ref.shape[0], taken_ref.shape[1] - 1
    carry = entering_ref[...]
    for block in range(blocks):
        out_ref[block] = carry.astype(BF16)
        carry = taken_ref[block, 0:pairs].astype(F32) + kept_of(taken_ref, block) * carry


def finish_kernel(within_ref, decayed_ref, incoming_ref, gain_ref, out_ref):
    dim = incoming_ref.shape[1]
    for head in range(incoming_ref.shape[0] // dim):
        span = pl.ds(head * dim, dim)
        carried = dot(decayed_ref[:, span], incoming_ref[span, :], (1, 0))
        attention = within_ref[:, span] + carried
        mean_square = jnp.mean(attention * attention, axis=1, keepdims=True)
        out_ref[:, span] = (attention * lax.rsqrt(mean_square + 1e-05) * gain_ref[:, span]).astype(BF16)


def params(mib=32):
    return pltpu.CompilerParams(vmem_limit_bytes=mib << 20)


def shards(query_rows, key_rows, value_rows, log_decay, lengths, norm_gain):
    rows, width = query_rows.shape
    heads = log_decay.shape[1]
    dim = width // heads
    holders = lax.axis_size("seq") // 4
    chains = [list(range(at, at + holders)) for at in range(0, 4 * holders, holders)]
    onward = [(holders + i, 2 * holders + i) for i in range(holders)]
    slots = width // holders
    pairs = slots // PAIR
    decay_rows = log_decay.T
    hbm = pl.BlockSpec(memory_space=pltpu.HBM)
    smem = pl.BlockSpec(memory_space=pltpu.SMEM)
    vmem = pl.BlockSpec(memory_space=pltpu.VMEM)

    states = pl.pallas_call(
        state_kernel,
        out_shape=jax.ShapeDtypeStruct((holders, pairs + 1, PAIR, dim), BF16),
        in_specs=[hbm, hbm, hbm, hbm],
        out_specs=vmem,
        scratch_shapes=[
            pltpu.SMEM(lengths.shape, lengths.dtype),
            pltpu.VMEM((rows, width), BF16),
            pltpu.VMEM((rows, width), BF16),
            pltpu.VMEM((heads, rows), F32),
            pltpu.SemaphoreType.DMA((2 * heads + 2,)),
        ],
        compiler_params=params(60),
        name="states",
    )(lengths, key_rows, value_rows, decay_rows)
    taken = lax.all_to_all(states, "seq", split_axis=0, concat_axis=0, tiled=True, axis_index_groups=chains)
    within, decayed, gain = pl.pallas_call(
        within_kernel,
        out_shape=(
            jax.ShapeDtypeStruct((rows, width), F32),
            jax.ShapeDtypeStruct((rows, width), BF16),
            jax.ShapeDtypeStruct((1, width), F32),
        ),
        in_specs=[smem, vmem, vmem, vmem, vmem, vmem],
        out_specs=(vmem, vmem, vmem),
        compiler_params=params(),
        cost_estimate=pl.CostEstimate(
            flops=4 * rows * rows * width, bytes_accessed=9 * rows * width, transcendentals=rows * rows * heads
        ),
        name="within",
    )(lengths, query_rows, key_rows, value_rows, decay_rows, norm_gain.reshape(1, width))
    total = pl.pallas_call(
        total_kernel,
        out_shape=jax.ShapeDtypeStruct((pairs, PAIR, dim), F32),
        in_specs=[vmem],
        out_specs=vmem,
        compiler_params=params(),
        name="total",
    )(taken)
    entering = lax.ppermute(total, "seq", onward)
    given = pl.pallas_call(
        scan_kernel,
        out_shape=jax.ShapeDtypeStruct((holders, pairs, PAIR, dim), BF16),
        in_specs=[vmem, vmem],
        out_specs=vmem,
        compiler_params=params(),
        name="scan",
    )(taken, entering)
    incoming = lax.all_to_all(given, "seq", split_axis=0, concat_axis=0, tiled=True, axis_index_groups=chains)
    normed = pl.pallas_call(
        finish_kernel,
        out_shape=jax.ShapeDtypeStruct((rows, width), BF16),
        in_specs=[vmem] * 4,
        out_specs=vmem,
        compiler_params=params(),
        name="finish",
    )(within, decayed, incoming.reshape(width, dim), gain)
    return lax.all_to_all(normed, "section", split_axis=0, concat_axis=1, tiled=True)


def solution(mesh):
    placed = (
        P("seq", "section"),
        P("seq", "section"),
        P("seq", "section"),
        P("seq", "section"),
        P(),
        P("section"),
    )
    return jax.shard_map(
        shards, mesh=mesh, in_specs=placed, out_specs=P(("seq", "section"), None), check_vma=False
    )
```

```python
import math

import jax
import jax.numpy as jnp
from jax import lax
from jax.experimental import pallas as pl
from jax.experimental.pallas import tpu as pltpu
from jax.sharding import PartitionSpec as P

F32, BF16 = jnp.float32, jnp.bfloat16
NEVER = -1e30
PAIR = 2
CHUNK = 128


def dot(a, b, contract):
    return lax.dot_general(a, b, ((contract[:1], contract[1:]), ((), ())), preferred_element_type=F32)


def three_parts(x):
    high = x.astype(BF16)
    rest = x - high.astype(F32)
    mid = rest.astype(BF16)
    return high, mid, (rest - mid.astype(F32)).astype(BF16)


def document_limits(lengths_ref, first_row, rows):
    last = first_row + rows - 1
    start_last, end_prev, begin = jnp.int32(0), jnp.int32(0), jnp.int32(0)
    found = jnp.bool_(False)
    for doc in range(lengths_ref.shape[0]):
        start_last = jnp.where(begin <= last, begin, start_last)
        end = begin + lengths_ref[doc]
        end_prev = jnp.where(found, end_prev, end)
        found = jnp.logical_or(found, end >= first_row)
        begin = end
    return start_last, end_prev


def state_kernel(lengths_hbm, key_hbm, value_hbm, decay_hbm, out_ref, lengths_ref, keys_ref, values_ref, decay_ref, sems):
    heads, rows = decay_ref.shape
    dim = keys_ref.shape[1] // heads
    holders, slots = out_ref.shape[0], heads * dim // out_ref.shape[0]
    chunks = rows // CHUNK
    small = [
        pltpu.make_async_copy(decay_hbm, decay_ref, sems.at[0]),
        pltpu.make_async_copy(lengths_hbm, lengths_ref, sems.at[1]),
    ]
    spans = [pl.ds(c * CHUNK, CHUNK) for c in range(chunks)]
    keys_in = [pltpu.make_async_copy(key_hbm.at[at], keys_ref.at[at], sems.at[2 + 2 * c]) for c, at in enumerate(spans)]
    values_in = [pltpu.make_async_copy(value_hbm.at[at], values_ref.at[at], sems.at[3 + 2 * c]) for c, at in enumerate(spans)]
    for copy in small:
        copy.start()
    for c in range(chunks):
        keys_in[c].start()
        values_in[c].start()
    row = lax.broadcasted_iota(jnp.int32, (CHUNK, CHUNK), 0)
    col = lax.broadcasted_iota(jnp.int32, (CHUNK, CHUNK), 1)
    later = (row > col).astype(F32).astype(BF16)
    small[0].wait()
    decay = jnp.concatenate([decay_ref[:, c * CHUNK : (c + 1) * CHUNK] for c in range(chunks)], axis=0)
    suffix = sum(dot(part, later, (1, 0)) for part in three_parts(decay))
    chunk_log = suffix[:, 0:1] + decay[:, 0:1]
    small[1].wait()
    first_row = lax.axis_index("seq") * rows
    start_last, _ = document_limits(lengths_ref, first_row, rows)
    scales = [None] * chunks
    end_log = jnp.zeros((heads, 1), F32)
    for c in reversed(range(chunks)):
        mine = slice(c * heads, (c + 1) * heads)
        position = first_row + c * CHUNK + lax.broadcasted_iota(jnp.int32, (1, CHUNK), 1)
        scales[c] = jnp.where(position >= start_last, jnp.exp(suffix[mine] + end_log), 0.0)
        end_log = end_log + chunk_log[mine]
    end_log = jnp.where(start_last >= first_row, NEVER, end_log)
    high, mid, low = (part.astype(F32) for part in three_parts(end_log))
    lane = lax.broadcasted_iota(jnp.int32, (PAIR, dim), 1)
    per_head = holders // heads
    scale = jnp.concatenate(scales, axis=1)
    for copy in keys_in + values_in:
        copy.wait()
    for head in range(heads):
        one = slice(head, head + 1)
        sent = jnp.where(lane == 0, high[one], jnp.where(lane == 1, mid[one], jnp.where(lane == 2, low[one], 0.0)))
        span = pl.ds(head * dim, dim)
        keys = (keys_ref[:, span].T.astype(F32) * scale[one, :]).astype(BF16)
        state = dot(keys, values_ref[:, span], (1, 0)).astype(BF16)
        for i in range(per_head):
            for pair in range(slots // PAIR):
                at = i * slots + pair * PAIR
                out_ref[head * per_head + i, pair] = state[at : at + PAIR, :]
            out_ref[head * per_head + i, slots // PAIR] = sent.astype(BF16)


def within_kernel(
    lengths_ref, query_hbm, key_hbm, value_hbm, decay_ref, gain_ref,
    within_ref, decayed_ref, staged_ref, query_ref, key_ref, value_ref, sems,
):
    heads, rows = decay_ref.shape
    fetched = [
        pltpu.make_async_copy(query_hbm, query_ref, sems.at[0]),
        pltpu.make_async_copy(key_hbm, key_ref, sems.at[1]),
        pltpu.make_async_copy(value_hbm, value_ref, sems.at[2]),
    ]
    for copy in fetched:
        copy.start()
    staged_ref[...] = gain_ref[...]
    dim = key_ref.shape[1] // heads
    scale = 1.0 / math.sqrt(dim)
    step = 128
    first_row = lax.axis_index("seq") * rows
    _, end_prev = document_limits(lengths_ref, first_row, rows)
    row = lax.broadcasted_iota(jnp.int32, (rows, rows), 0)
    col = lax.broadcasted_iota(jnp.int32, (rows, rows), 1)
    upto = (col <= row).astype(F32).astype(BF16)
    parts = three_parts(decay_ref[...])
    cumul_col = sum(dot(upto, part, (1, 1)) for part in parts)
    cumul_row = sum(dot(part, upto, (1, 1)) for part in parts)
    spot_row = first_row + lax.broadcasted_iota(jnp.int32, (1, rows), 1)
    lane = lax.broadcasted_iota(jnp.int32, (1, dim), 1)
    doc_row = jnp.zeros((1, rows), F32)
    ends = jnp.zeros((1, dim), jnp.int32)
    end = jnp.int32(0)
    for doc in range(lengths_ref.shape[0]):
        end = end + lengths_ref[doc]
        doc_row = doc_row + jnp.where(spot_row >= end, 1.0, 0.0)
        ends = ends + jnp.where(lane >= doc, lengths_ref[doc], 0)
    position = first_row + lax.broadcasted_iota(jnp.int32, (rows, 1), 0)
    doc_col = jnp.sum(jnp.where(ends <= position, 1.0, 0.0), axis=1, keepdims=True)
    for copy in fetched:
        copy.wait()
    query_scale = jnp.where(position < end_prev, jnp.exp(cumul_col) * scale, 0.0)
    for head in range(heads):
        span = pl.ds(head * dim, dim)
        decayed_ref[:, span] = (query_ref[:, span].astype(F32) * query_scale[:, head : head + 1]).astype(BF16)
    for at in range(0, rows, step):
        upper = at + step
        t = at + lax.broadcasted_iota(jnp.int32, (step, upper), 0)
        u = lax.broadcasted_iota(jnp.int32, (step, upper), 1)
        allowed = jnp.logical_and(u <= t, doc_col[at:upper] == doc_row[:, :upper])
        shut = jnp.where(allowed, 0.0, NEVER)
        for head in range(heads):
            span = pl.ds(head * dim, dim)
            scores = dot(query_ref[pl.ds(at, step), span], key_ref[pl.ds(0, upper), span], (1, 1))
            gap = cumul_col[at:upper, head : head + 1] - cumul_row[head : head + 1, :upper]
            weights = jnp.where(allowed, scores * scale * jnp.exp(jnp.minimum(gap, 0.0) + shut), 0.0).astype(BF16)
            within_ref[pl.ds(at, step), span] = dot(weights, value_ref[pl.ds(0, upper), span], (1, 0))


def kept_of(taken_ref, block):
    parts = taken_ref[block, taken_ref.shape[1] - 1].astype(F32)[0:1, 0:3]
    return jnp.exp(jnp.sum(parts, axis=1, keepdims=True))


def total_kernel(taken_ref, total_ref):
    blocks, pairs = taken_ref.shape[0], taken_ref.shape[1] - 1
    carry = jnp.zeros(total_ref.shape, F32)
    for block in range(blocks):
        carry = taken_ref[block, 0:pairs].astype(F32) + kept_of(taken_ref, block) * carry
    total_ref[...] = carry


def prefix_kernel(taken_ref, before_ref, reach_ref):
    blocks, pairs = taken_ref.shape[0], taken_ref.shape[1] - 1
    carry = jnp.zeros(before_ref.shape[1:], F32)
    reach = jnp.ones((1, 1), F32)
    for block in range(blocks):
        before_ref[block] = carry
        reach_ref[block] = jnp.broadcast_to(reach, reach_ref.shape[1:])
        kept = kept_of(taken_ref, block)
        carry = taken_ref[block, 0:pairs].astype(F32) + kept * carry
        reach = kept * reach


def enter_kernel(before_ref, reach_ref, entering_ref, out_ref):
    slots = entering_ref.shape[0]
    entering = entering_ref[...]
    for block in range(out_ref.shape[0]):
        at = pl.ds(block * slots, slots)
        reach = reach_ref[block * PAIR : block * PAIR + 1, :]
        out_ref[block] = (before_ref[at, :] + reach * entering).astype(BF16)


def finish_kernel(within_ref, decayed_ref, incoming_ref, gain_ref, out_ref):
    dim = incoming_ref.shape[1]
    for head in range(incoming_ref.shape[0] // dim):
        span = pl.ds(head * dim, dim)
        carried = dot(decayed_ref[:, span], incoming_ref[span, :], (1, 0))
        attention = within_ref[:, span] + carried
        mean_square = jnp.mean(attention * attention, axis=1, keepdims=True)
        out_ref[:, span] = (attention * lax.rsqrt(mean_square + 1e-05) * gain_ref[:, span]).astype(BF16)


def params():
    return pltpu.CompilerParams(vmem_limit_bytes=32 << 20)


def in_hbm(x):
    return pltpu.with_memory_space_constraint(x, pltpu.HBM)


def shards(query_rows, key_rows, value_rows, log_decay, lengths, norm_gain):
    rows, width = query_rows.shape
    heads = log_decay.shape[1]
    dim = width // heads
    holders = lax.axis_size("seq") // 4
    chains = [list(range(at, at + holders)) for at in range(0, 4 * holders, holders)]
    onward = [(holders + i, 2 * holders + i) for i in range(holders)]
    slots = width // holders
    pairs = slots // PAIR
    decay_rows = log_decay.T
    hbm = pl.BlockSpec(memory_space=pltpu.HBM)
    smem = pl.BlockSpec(memory_space=pltpu.SMEM)
    vmem = pl.BlockSpec(memory_space=pltpu.VMEM)

    states = pl.pallas_call(
        state_kernel,
        out_shape=jax.ShapeDtypeStruct((holders, pairs + 1, PAIR, dim), BF16),
        in_specs=[hbm, hbm, hbm, hbm],
        out_specs=vmem,
        scratch_shapes=[
            pltpu.SMEM(lengths.shape, lengths.dtype),
            pltpu.VMEM((rows, width), BF16),
            pltpu.VMEM((rows, width), BF16),
            pltpu.VMEM((heads, rows), F32),
            pltpu.SemaphoreType.DMA((2 * (rows // CHUNK) + 2,)),
        ],
        compiler_params=params(),
        name="states",
    )(*(in_hbm(x) for x in (lengths, key_rows, value_rows, decay_rows)))
    taken = lax.all_to_all(states, "seq", split_axis=0, concat_axis=0, tiled=True, axis_index_groups=chains)
    within, decayed, gain = pl.pallas_call(
        within_kernel,
        out_shape=(
            jax.ShapeDtypeStruct((rows, width), F32),
            jax.ShapeDtypeStruct((rows, width), BF16),
            jax.ShapeDtypeStruct((1, width), F32),
        ),
        in_specs=[smem, hbm, hbm, hbm, vmem, vmem],
        out_specs=(vmem, vmem, vmem),
        scratch_shapes=[pltpu.VMEM((rows, width), BF16)] * 3 + [pltpu.SemaphoreType.DMA((3,))],
        compiler_params=params(),
        cost_estimate=pl.CostEstimate(
            flops=4 * rows * rows * width, bytes_accessed=9 * rows * width, transcendentals=rows * rows * heads
        ),
        name="within",
    )(lengths, *(in_hbm(x) for x in (query_rows, key_rows, value_rows)), decay_rows, norm_gain.reshape(1, width))
    taken, within, decayed, gain = lax.optimization_barrier((taken, within, decayed, gain))
    total = pl.pallas_call(
        total_kernel,
        out_shape=jax.ShapeDtypeStruct((pairs, PAIR, dim), F32),
        in_specs=[vmem],
        out_specs=vmem,
        compiler_params=params(),
        name="total",
    )(taken)
    entering = lax.ppermute(total, "seq", onward)
    before, reach = pl.pallas_call(
        prefix_kernel,
        out_shape=(
            jax.ShapeDtypeStruct((holders, pairs, PAIR, dim), F32),
            jax.ShapeDtypeStruct((holders, PAIR, dim), F32),
        ),
        in_specs=[vmem],
        out_specs=(vmem, vmem),
        compiler_params=params(),
        cost_estimate=pl.CostEstimate(flops=2 * width * dim, bytes_accessed=6 * width * dim, transcendentals=holders),
        name="prefix",
    )(taken)
    given = pl.pallas_call(
        enter_kernel,
        out_shape=jax.ShapeDtypeStruct((holders, slots, dim), BF16),
        in_specs=[vmem] * 3,
        out_specs=vmem,
        compiler_params=params(),
        name="enter",
    )(before.reshape(width, dim), reach.reshape(holders * PAIR, dim), entering.reshape(slots, dim))
    incoming = lax.all_to_all(given, "seq", split_axis=0, concat_axis=0, tiled=True, axis_index_groups=chains)
    normed = pl.pallas_call(
        finish_kernel,
        out_shape=jax.ShapeDtypeStruct((rows, width), BF16),
        in_specs=[vmem] * 4,
        out_specs=vmem,
        compiler_params=params(),
        name="finish",
    )(within, decayed, incoming.reshape(width, dim), gain)
    return lax.all_to_all(normed, "section", split_axis=0, concat_axis=1, tiled=True)


def solution(mesh):
    placed = (
        P("seq", "section"),
        P("seq", "section"),
        P("seq", "section"),
        P("seq", "section"),
        P(),
        P("section"),
    )
    return jax.shard_map(
        shards, mesh=mesh, in_specs=placed, out_specs=P(("seq", "section"), None), check_vma=False
    )
```

```python
import functools
import math

import jax
import jax.numpy as jnp
from jax import lax
from jax.experimental import pallas as pl
from jax.experimental.pallas import tpu as pltpu
from jax.sharding import PartitionSpec as P

F32, BF16 = jnp.float32, jnp.bfloat16
NEVER = -1e30
PAIR = 2
CHUNK = 128
FIRST_Z = 8
FIRST_SECTION = 4


def place(position, count):
    return (position + FIRST_Z) % count


def in_chain(count):
    return sorted(range(count), key=lambda position: place(position, count))


def dot(a, b, contract):
    return lax.dot_general(a, b, ((contract[:1], contract[1:]), ((), ())), preferred_element_type=F32)


def three_parts(x):
    high = x.astype(BF16)
    rest = x - high.astype(F32)
    mid = rest.astype(BF16)
    return high, mid, (rest - mid.astype(F32)).astype(BF16)


def document_limits(lengths_ref, first_row, rows):
    last = first_row + rows - 1
    start_last, end_prev, begin = jnp.int32(0), jnp.int32(0), jnp.int32(0)
    found = jnp.bool_(False)
    for doc in range(lengths_ref.shape[0]):
        start_last = jnp.where(begin <= last, begin, start_last)
        end = begin + lengths_ref[doc]
        end_prev = jnp.where(found, end_prev, end)
        found = jnp.logical_or(found, end >= first_row)
        begin = end
    return start_last, end_prev


def state_kernel(lengths_hbm, key_hbm, value_hbm, decay_hbm, out_ref, lengths_ref, keys_ref, values_ref, decay_ref, sems):
    heads, rows = decay_ref.shape
    dim = keys_ref.shape[1] // heads
    holders, slots = out_ref.shape[0], heads * dim // out_ref.shape[0]
    chunks = rows // CHUNK
    small = [
        pltpu.make_async_copy(decay_hbm, decay_ref, sems.at[0]),
        pltpu.make_async_copy(lengths_hbm, lengths_ref, sems.at[1]),
    ]
    spans = [pl.ds(c * CHUNK, CHUNK) for c in range(chunks)]
    keys_in = [pltpu.make_async_copy(key_hbm.at[at], keys_ref.at[at], sems.at[2 + 2 * c]) for c, at in enumerate(spans)]
    values_in = [pltpu.make_async_copy(value_hbm.at[at], values_ref.at[at], sems.at[3 + 2 * c]) for c, at in enumerate(spans)]
    for copy in small:
        copy.start()
    for c in range(chunks):
        keys_in[c].start()
        values_in[c].start()
    row = lax.broadcasted_iota(jnp.int32, (CHUNK, CHUNK), 0)
    col = lax.broadcasted_iota(jnp.int32, (CHUNK, CHUNK), 1)
    later = (row > col).astype(F32).astype(BF16)
    small[0].wait()
    decay = jnp.concatenate([decay_ref[:, c * CHUNK : (c + 1) * CHUNK] for c in range(chunks)], axis=0)
    suffix = sum(dot(part, later, (1, 0)) for part in three_parts(decay))
    chunk_log = suffix[:, 0:1] + decay[:, 0:1]
    small[1].wait()
    first_row = lax.axis_index("seq") * rows
    start_last, _ = document_limits(lengths_ref, first_row, rows)
    scales = [None] * chunks
    end_log = jnp.zeros((heads, 1), F32)
    for c in reversed(range(chunks)):
        mine = slice(c * heads, (c + 1) * heads)
        position = first_row + c * CHUNK + lax.broadcasted_iota(jnp.int32, (1, CHUNK), 1)
        scales[c] = jnp.where(position >= start_last, jnp.exp(suffix[mine] + end_log), 0.0)
        end_log = end_log + chunk_log[mine]
    end_log = jnp.where(start_last >= first_row, NEVER, end_log)
    high, mid, low = (part.astype(F32) for part in three_parts(end_log))
    lane = lax.broadcasted_iota(jnp.int32, (PAIR, dim), 1)
    per_head = holders // heads
    scale = jnp.concatenate(scales, axis=1)
    for copy in keys_in + values_in:
        copy.wait()
    for head in range(heads):
        one = slice(head, head + 1)
        sent = jnp.where(lane == 0, high[one], jnp.where(lane == 1, mid[one], jnp.where(lane == 2, low[one], 0.0)))
        span = pl.ds(head * dim, dim)
        keys = (keys_ref[:, span].T.astype(F32) * scale[one, :]).astype(BF16)
        state = dot(keys, values_ref[:, span], (1, 0)).astype(BF16)
        for i in range(per_head):
            for pair in range(slots // PAIR):
                at = i * slots + pair * PAIR
                out_ref[head * per_head + i, pair] = state[at : at + PAIR, :]
            out_ref[head * per_head + i, slots // PAIR] = sent.astype(BF16)


def within_kernel(
    lengths_ref, query_hbm, key_hbm, value_hbm, decay_ref, gain_ref,
    within_ref, decayed_ref, staged_ref, query_ref, key_ref, value_ref, sems,
):
    heads, rows = decay_ref.shape
    fetched = [
        pltpu.make_async_copy(query_hbm, query_ref, sems.at[0]),
        pltpu.make_async_copy(key_hbm, key_ref, sems.at[1]),
        pltpu.make_async_copy(value_hbm, value_ref, sems.at[2]),
    ]
    for copy in fetched:
        copy.start()
    staged_ref[...] = gain_ref[...]
    dim = key_ref.shape[1] // heads
    scale = 1.0 / math.sqrt(dim)
    step = 128
    first_row = lax.axis_index("seq") * rows
    _, end_prev = document_limits(lengths_ref, first_row, rows)
    row = lax.broadcasted_iota(jnp.int32, (rows, rows), 0)
    col = lax.broadcasted_iota(jnp.int32, (rows, rows), 1)
    upto = (col <= row).astype(F32).astype(BF16)
    parts = three_parts(decay_ref[...])
    cumul_col = sum(dot(upto, part, (1, 1)) for part in parts)
    cumul_row = sum(dot(part, upto, (1, 1)) for part in parts)
    spot_row = first_row + lax.broadcasted_iota(jnp.int32, (1, rows), 1)
    lane = lax.broadcasted_iota(jnp.int32, (1, dim), 1)
    doc_row = jnp.zeros((1, rows), F32)
    ends = jnp.zeros((1, dim), jnp.int32)
    end = jnp.int32(0)
    for doc in range(lengths_ref.shape[0]):
        end = end + lengths_ref[doc]
        doc_row = doc_row + jnp.where(spot_row >= end, 1.0, 0.0)
        ends = ends + jnp.where(lane >= doc, lengths_ref[doc], 0)
    position = first_row + lax.broadcasted_iota(jnp.int32, (rows, 1), 0)
    doc_col = jnp.sum(jnp.where(ends <= position, 1.0, 0.0), axis=1, keepdims=True)
    for copy in fetched:
        copy.wait()
    query_scale = jnp.where(position < end_prev, jnp.exp(cumul_col) * scale, 0.0)
    for head in range(heads):
        span = pl.ds(head * dim, dim)
        decayed_ref[:, span] = (query_ref[:, span].astype(F32) * query_scale[:, head : head + 1]).astype(BF16)
    for at in range(0, rows, step):
        upper = at + step
        t = at + lax.broadcasted_iota(jnp.int32, (step, upper), 0)
        u = lax.broadcasted_iota(jnp.int32, (step, upper), 1)
        allowed = jnp.logical_and(u <= t, doc_col[at:upper] == doc_row[:, :upper])
        shut = jnp.where(allowed, 0.0, NEVER)
        for head in range(heads):
            span = pl.ds(head * dim, dim)
            scores = dot(query_ref[pl.ds(at, step), span], key_ref[pl.ds(0, upper), span], (1, 1))
            gap = cumul_col[at:upper, head : head + 1] - cumul_row[head : head + 1, :upper]
            weights = jnp.where(allowed, scores * scale * jnp.exp(jnp.minimum(gap, 0.0) + shut), 0.0).astype(BF16)
            within_ref[pl.ds(at, step), span] = dot(weights, value_ref[pl.ds(0, upper), span], (1, 0))


def kept_of(taken_ref, block):
    parts = taken_ref[block, taken_ref.shape[1] - 1].astype(F32)[0:1, 0:3]
    return jnp.exp(jnp.sum(parts, axis=1, keepdims=True))


def total_kernel(taken_ref, total_ref):
    blocks, pairs = taken_ref.shape[0], taken_ref.shape[1] - 1
    carry = jnp.zeros(total_ref.shape, F32)
    for block in in_chain(blocks):
        carry = taken_ref[block, 0:pairs].astype(F32) + kept_of(taken_ref, block) * carry
    total_ref[...] = carry


def prefix_kernel(taken_ref, before_ref, reach_ref):
    blocks, pairs = taken_ref.shape[0], taken_ref.shape[1] - 1
    carry = jnp.zeros(before_ref.shape[1:], F32)
    reach = jnp.ones((1, 1), F32)
    for block in in_chain(blocks):
        before_ref[block] = carry
        reach_ref[block] = jnp.broadcast_to(reach, reach_ref.shape[1:])
        kept = kept_of(taken_ref, block)
        carry = taken_ref[block, 0:pairs].astype(F32) + kept * carry
        reach = kept * reach


def enter_kernel(before_ref, reach_ref, entering_ref, out_ref):
    slots = entering_ref.shape[0]
    entering = entering_ref[...]
    for block in range(out_ref.shape[0]):
        at = pl.ds(block * slots, slots)
        reach = reach_ref[block * PAIR : block * PAIR + 1, :]
        out_ref[block] = (before_ref[at, :] + reach * entering).astype(BF16)


def finish_kernel(sections, within_ref, decayed_ref, incoming_ref, gain_ref, out_ref):
    dim = incoming_ref.shape[1]
    tokens = out_ref.shape[1]
    for head in range(incoming_ref.shape[0] // dim):
        span = pl.ds(head * dim, dim)
        carried = dot(decayed_ref[:, span], incoming_ref[span, :], (1, 0))
        attention = within_ref[:, span] + carried
        mean_square = jnp.mean(attention * attention, axis=1, keepdims=True)
        normed = (attention * lax.rsqrt(mean_square + 1e-05) * gain_ref[:, span]).astype(BF16)
        for i, section in enumerate(sections):
            out_ref[i, :, span] = normed[section * tokens : (section + 1) * tokens, :]


def place_kernel(sections, landed_ref, out_hbm, sems):
    width = landed_ref.shape[2]
    copies = [
        pltpu.make_async_copy(landed_ref.at[i], out_hbm.at[:, pl.ds(section * width, width)], sems.at[i])
        for i, section in enumerate(sections)
    ]
    for copy in copies:
        copy.start()
    for copy in copies:
        copy.wait()


def params():
    return pltpu.CompilerParams(vmem_limit_bytes=32 << 20)


def in_hbm(x):
    return pltpu.with_memory_space_constraint(x, pltpu.HBM)


def shards(query_rows, key_rows, value_rows, log_decay, lengths, norm_gain):
    rows, width = query_rows.shape
    heads = log_decay.shape[1]
    dim = width // heads
    holders = lax.axis_size("seq") // 4
    chains = [[at + place(i, holders) for i in range(holders)] for at in range(0, 4 * holders, holders)]
    onward = [(holders + i, 2 * holders + i) for i in range(holders)]
    slots = width // holders
    pairs = slots // PAIR
    decay_rows = log_decay.T
    hbm = pl.BlockSpec(memory_space=pltpu.HBM)
    smem = pl.BlockSpec(memory_space=pltpu.SMEM)
    vmem = pl.BlockSpec(memory_space=pltpu.VMEM)

    states = pl.pallas_call(
        state_kernel,
        out_shape=jax.ShapeDtypeStruct((holders, pairs + 1, PAIR, dim), BF16),
        in_specs=[hbm, hbm, hbm, hbm],
        out_specs=vmem,
        scratch_shapes=[
            pltpu.SMEM(lengths.shape, lengths.dtype),
            pltpu.VMEM((rows, width), BF16),
            pltpu.VMEM((rows, width), BF16),
            pltpu.VMEM((heads, rows), F32),
            pltpu.SemaphoreType.DMA((2 * (rows // CHUNK) + 2,)),
        ],
        compiler_params=params(),
        name="states",
    )(*(in_hbm(x) for x in (lengths, key_rows, value_rows, decay_rows)))
    taken = lax.all_to_all(states, "seq", split_axis=0, concat_axis=0, tiled=True, axis_index_groups=chains)
    within, decayed, gain = pl.pallas_call(
        within_kernel,
        out_shape=(
            jax.ShapeDtypeStruct((rows, width), F32),
            jax.ShapeDtypeStruct((rows, width), BF16),
            jax.ShapeDtypeStruct((1, width), F32),
        ),
        in_specs=[smem, hbm, hbm, hbm, vmem, vmem],
        out_specs=(vmem, vmem, vmem),
        scratch_shapes=[pltpu.VMEM((rows, width), BF16)] * 3 + [pltpu.SemaphoreType.DMA((3,))],
        compiler_params=params(),
        cost_estimate=pl.CostEstimate(
            flops=4 * rows * rows * width, bytes_accessed=9 * rows * width, transcendentals=rows * rows * heads
        ),
        name="within",
    )(lengths, *(in_hbm(x) for x in (query_rows, key_rows, value_rows)), decay_rows, norm_gain.reshape(1, width))
    taken, within, decayed, gain = lax.optimization_barrier((taken, within, decayed, gain))
    total = pl.pallas_call(
        total_kernel,
        out_shape=jax.ShapeDtypeStruct((pairs, PAIR, dim), F32),
        in_specs=[vmem],
        out_specs=vmem,
        compiler_params=params(),
        name="total",
    )(taken)
    entering = lax.ppermute(total, "seq", onward)
    before, reach = pl.pallas_call(
        prefix_kernel,
        out_shape=(
            jax.ShapeDtypeStruct((holders, pairs, PAIR, dim), F32),
            jax.ShapeDtypeStruct((holders, PAIR, dim), F32),
        ),
        in_specs=[vmem],
        out_specs=(vmem, vmem),
        compiler_params=params(),
        cost_estimate=pl.CostEstimate(flops=2 * width * dim, bytes_accessed=6 * width * dim, transcendentals=holders),
        name="prefix",
    )(taken)
    given = pl.pallas_call(
        enter_kernel,
        out_shape=jax.ShapeDtypeStruct((holders, slots, dim), BF16),
        in_specs=[vmem] * 3,
        out_specs=vmem,
        compiler_params=params(),
        name="enter",
    )(before.reshape(width, dim), reach.reshape(holders * PAIR, dim), entering.reshape(slots, dim))
    incoming = lax.all_to_all(given, "seq", split_axis=0, concat_axis=0, tiled=True, axis_index_groups=chains)
    count = lax.axis_size("section")
    sections = [(i + FIRST_SECTION) % count for i in range(count)]
    normed = pl.pallas_call(
        functools.partial(finish_kernel, sections),
        out_shape=jax.ShapeDtypeStruct((count, rows // count, width), BF16),
        in_specs=[vmem] * 4,
        out_specs=vmem,
        compiler_params=params(),
        name="finish",
    )(within, decayed, incoming.reshape(width, dim), gain)
    landed = lax.all_to_all(
        normed, "section", split_axis=0, concat_axis=0, tiled=True, axis_index_groups=[sections]
    )
    return pl.pallas_call(
        functools.partial(place_kernel, sections),
        out_shape=jax.ShapeDtypeStruct((rows // count, count * width), BF16),
        in_specs=[vmem],
        out_specs=hbm,
        scratch_shapes=[pltpu.SemaphoreType.DMA((count,))],
        compiler_params=params(),
        name="place",
    )(landed)


def solution(mesh):
    placed = (
        P("seq", "section"),
        P("seq", "section"),
        P("seq", "section"),
        P("seq", "section"),
        P(),
        P("section"),
    )
    return jax.shard_map(
        shards, mesh=mesh, in_specs=placed, out_specs=P(("seq", "section"), None), check_vma=False
    )
```

```python
import functools
import math

import jax
import jax.numpy as jnp
from jax import lax
from jax.experimental import pallas as pl
from jax.experimental.pallas import tpu as pltpu
from jax.sharding import PartitionSpec as P

F32, BF16 = jnp.float32, jnp.bfloat16
NEVER = -1e30
PAIR = 2
CHUNK = 128
ORDER_Z = (8, 7, 6, 5, 4, 3, 2, 1, 0, 15, 14, 13, 12, 11, 10, 9)
ORDER_SECTION = (5, 4, 7, 6, 1, 0, 3, 2)


def in_chain(count):
    return sorted(range(count), key=lambda position: ORDER_Z[position])


def dot(a, b, contract):
    return lax.dot_general(a, b, ((contract[:1], contract[1:]), ((), ())), preferred_element_type=F32)


def three_parts(x):
    high = x.astype(BF16)
    rest = x - high.astype(F32)
    mid = rest.astype(BF16)
    return high, mid, (rest - mid.astype(F32)).astype(BF16)


def document_limits(lengths_ref, first_row, rows):
    last = first_row + rows - 1
    start_last, end_prev, begin = jnp.int32(0), jnp.int32(0), jnp.int32(0)
    found = jnp.bool_(False)
    for doc in range(lengths_ref.shape[0]):
        start_last = jnp.where(begin <= last, begin, start_last)
        end = begin + lengths_ref[doc]
        end_prev = jnp.where(found, end_prev, end)
        found = jnp.logical_or(found, end >= first_row)
        begin = end
    return start_last, end_prev


def state_kernel(lengths_hbm, key_hbm, value_hbm, decay_hbm, out_ref, lengths_ref, keys_ref, values_ref, decay_ref, sems):
    heads, rows = decay_ref.shape
    dim = keys_ref.shape[1] // heads
    holders, slots = out_ref.shape[0], heads * dim // out_ref.shape[0]
    chunks = rows // CHUNK
    small = [
        pltpu.make_async_copy(decay_hbm, decay_ref, sems.at[0]),
        pltpu.make_async_copy(lengths_hbm, lengths_ref, sems.at[1]),
    ]
    spans = [pl.ds(c * CHUNK, CHUNK) for c in range(chunks)]
    keys_in = [pltpu.make_async_copy(key_hbm.at[at], keys_ref.at[at], sems.at[2 + 2 * c]) for c, at in enumerate(spans)]
    values_in = [pltpu.make_async_copy(value_hbm.at[at], values_ref.at[at], sems.at[3 + 2 * c]) for c, at in enumerate(spans)]
    for copy in small:
        copy.start()
    for c in range(chunks):
        keys_in[c].start()
        values_in[c].start()
    row = lax.broadcasted_iota(jnp.int32, (CHUNK, CHUNK), 0)
    col = lax.broadcasted_iota(jnp.int32, (CHUNK, CHUNK), 1)
    later = (row > col).astype(F32).astype(BF16)
    small[0].wait()
    decay = jnp.concatenate([decay_ref[:, c * CHUNK : (c + 1) * CHUNK] for c in range(chunks)], axis=0)
    suffix = sum(dot(part, later, (1, 0)) for part in three_parts(decay))
    chunk_log = suffix[:, 0:1] + decay[:, 0:1]
    small[1].wait()
    first_row = lax.axis_index("seq") * rows
    start_last, _ = document_limits(lengths_ref, first_row, rows)
    scales = [None] * chunks
    end_log = jnp.zeros((heads, 1), F32)
    for c in reversed(range(chunks)):
        mine = slice(c * heads, (c + 1) * heads)
        position = first_row + c * CHUNK + lax.broadcasted_iota(jnp.int32, (1, CHUNK), 1)
        scales[c] = jnp.where(position >= start_last, jnp.exp(suffix[mine] + end_log), 0.0)
        end_log = end_log + chunk_log[mine]
    end_log = jnp.where(start_last >= first_row, NEVER, end_log)
    high, mid, low = (part.astype(F32) for part in three_parts(end_log))
    lane = lax.broadcasted_iota(jnp.int32, (PAIR, dim), 1)
    per_head = holders // heads
    scale = jnp.concatenate(scales, axis=1)
    for copy in keys_in + values_in:
        copy.wait()
    for head in range(heads):
        one = slice(head, head + 1)
        sent = jnp.where(lane == 0, high[one], jnp.where(lane == 1, mid[one], jnp.where(lane == 2, low[one], 0.0)))
        span = pl.ds(head * dim, dim)
        keys = (keys_ref[:, span].T.astype(F32) * scale[one, :]).astype(BF16)
        state = dot(keys, values_ref[:, span], (1, 0)).astype(BF16)
        for i in range(per_head):
            for pair in range(slots // PAIR):
                at = i * slots + pair * PAIR
                out_ref[head * per_head + i, pair] = state[at : at + PAIR, :]
            out_ref[head * per_head + i, slots // PAIR] = sent.astype(BF16)


def within_kernel(
    lengths_ref, query_hbm, key_hbm, value_hbm, decay_ref, gain_ref,
    within_ref, decayed_ref, staged_ref, query_ref, key_ref, value_ref, sems,
):
    heads, rows = decay_ref.shape
    fetched = [
        pltpu.make_async_copy(query_hbm, query_ref, sems.at[0]),
        pltpu.make_async_copy(key_hbm, key_ref, sems.at[1]),
        pltpu.make_async_copy(value_hbm, value_ref, sems.at[2]),
    ]
    for copy in fetched:
        copy.start()
    staged_ref[...] = gain_ref[...]
    dim = key_ref.shape[1] // heads
    scale = 1.0 / math.sqrt(dim)
    step = 128
    first_row = lax.axis_index("seq") * rows
    _, end_prev = document_limits(lengths_ref, first_row, rows)
    row = lax.broadcasted_iota(jnp.int32, (rows, rows), 0)
    col = lax.broadcasted_iota(jnp.int32, (rows, rows), 1)
    upto = (col <= row).astype(F32).astype(BF16)
    parts = three_parts(decay_ref[...])
    cumul_col = sum(dot(upto, part, (1, 1)) for part in parts)
    cumul_row = sum(dot(part, upto, (1, 1)) for part in parts)
    spot_row = first_row + lax.broadcasted_iota(jnp.int32, (1, rows), 1)
    lane = lax.broadcasted_iota(jnp.int32, (1, dim), 1)
    doc_row = jnp.zeros((1, rows), F32)
    ends = jnp.zeros((1, dim), jnp.int32)
    end = jnp.int32(0)
    for doc in range(lengths_ref.shape[0]):
        end = end + lengths_ref[doc]
        doc_row = doc_row + jnp.where(spot_row >= end, 1.0, 0.0)
        ends = ends + jnp.where(lane >= doc, lengths_ref[doc], 0)
    position = first_row + lax.broadcasted_iota(jnp.int32, (rows, 1), 0)
    doc_col = jnp.sum(jnp.where(ends <= position, 1.0, 0.0), axis=1, keepdims=True)
    for copy in fetched:
        copy.wait()
    query_scale = jnp.where(position < end_prev, jnp.exp(cumul_col) * scale, 0.0)
    for head in range(heads):
        span = pl.ds(head * dim, dim)
        decayed_ref[:, span] = (query_ref[:, span].astype(F32) * query_scale[:, head : head + 1]).astype(BF16)
    for at in range(0, rows, step):
        upper = at + step
        t = at + lax.broadcasted_iota(jnp.int32, (step, upper), 0)
        u = lax.broadcasted_iota(jnp.int32, (step, upper), 1)
        allowed = jnp.logical_and(u <= t, doc_col[at:upper] == doc_row[:, :upper])
        shut = jnp.where(allowed, 0.0, NEVER)
        for head in range(heads):
            span = pl.ds(head * dim, dim)
            scores = dot(query_ref[pl.ds(at, step), span], key_ref[pl.ds(0, upper), span], (1, 1))
            gap = cumul_col[at:upper, head : head + 1] - cumul_row[head : head + 1, :upper]
            weights = jnp.where(allowed, scores * scale * jnp.exp(jnp.minimum(gap, 0.0) + shut), 0.0).astype(BF16)
            within_ref[pl.ds(at, step), span] = dot(weights, value_ref[pl.ds(0, upper), span], (1, 0))


def kept_of(taken_ref, block):
    parts = taken_ref[block, taken_ref.shape[1] - 1].astype(F32)[0:1, 0:3]
    return jnp.exp(jnp.sum(parts, axis=1, keepdims=True))


def total_kernel(taken_ref, total_ref):
    blocks, pairs = taken_ref.shape[0], taken_ref.shape[1] - 1
    carry = jnp.zeros(total_ref.shape, F32)
    for block in in_chain(blocks):
        carry = taken_ref[block, 0:pairs].astype(F32) + kept_of(taken_ref, block) * carry
    total_ref[...] = carry


def prefix_kernel(taken_ref, before_ref, reach_ref):
    blocks, pairs = taken_ref.shape[0], taken_ref.shape[1] - 1
    carry = jnp.zeros(before_ref.shape[1:], F32)
    reach = jnp.ones((1, 1), F32)
    for block in in_chain(blocks):
        before_ref[block] = carry
        reach_ref[block] = jnp.broadcast_to(reach, reach_ref.shape[1:])
        kept = kept_of(taken_ref, block)
        carry = taken_ref[block, 0:pairs].astype(F32) + kept * carry
        reach = kept * reach


def enter_kernel(before_ref, reach_ref, entering_ref, out_ref):
    slots = entering_ref.shape[0]
    entering = entering_ref[...]
    for block in range(out_ref.shape[0]):
        at = pl.ds(block * slots, slots)
        reach = reach_ref[block * PAIR : block * PAIR + 1, :]
        out_ref[block] = (before_ref[at, :] + reach * entering).astype(BF16)


def finish_kernel(sections, within_ref, decayed_ref, incoming_ref, gain_ref, out_ref):
    dim = incoming_ref.shape[1]
    tokens = out_ref.shape[1]
    for head in range(incoming_ref.shape[0] // dim):
        span = pl.ds(head * dim, dim)
        carried = dot(decayed_ref[:, span], incoming_ref[span, :], (1, 0))
        attention = within_ref[:, span] + carried
        mean_square = jnp.mean(attention * attention, axis=1, keepdims=True)
        normed = (attention * lax.rsqrt(mean_square + 1e-05) * gain_ref[:, span]).astype(BF16)
        for i, section in enumerate(sections):
            out_ref[i, :, span] = normed[section * tokens : (section + 1) * tokens, :]


def place_kernel(sections, landed_ref, out_hbm, sems):
    width = landed_ref.shape[2]
    copies = [
        pltpu.make_async_copy(landed_ref.at[i], out_hbm.at[:, pl.ds(section * width, width)], sems.at[i])
        for i, section in enumerate(sections)
    ]
    for copy in copies:
        copy.start()
    for copy in copies:
        copy.wait()


def params():
    return pltpu.CompilerParams(vmem_limit_bytes=32 << 20)


def in_hbm(x):
    return pltpu.with_memory_space_constraint(x, pltpu.HBM)


def shards(query_rows, key_rows, value_rows, log_decay, lengths, norm_gain):
    rows, width = query_rows.shape
    heads = log_decay.shape[1]
    dim = width // heads
    holders = lax.axis_size("seq") // 4
    chains = [[at + z for z in ORDER_Z] for at in range(0, 4 * holders, holders)]
    onward = [(holders + i, 2 * holders + i) for i in range(holders)]
    slots = width // holders
    pairs = slots // PAIR
    decay_rows = log_decay.T
    hbm = pl.BlockSpec(memory_space=pltpu.HBM)
    smem = pl.BlockSpec(memory_space=pltpu.SMEM)
    vmem = pl.BlockSpec(memory_space=pltpu.VMEM)

    states = pl.pallas_call(
        state_kernel,
        out_shape=jax.ShapeDtypeStruct((holders, pairs + 1, PAIR, dim), BF16),
        in_specs=[hbm, hbm, hbm, hbm],
        out_specs=vmem,
        scratch_shapes=[
            pltpu.SMEM(lengths.shape, lengths.dtype),
            pltpu.VMEM((rows, width), BF16),
            pltpu.VMEM((rows, width), BF16),
            pltpu.VMEM((heads, rows), F32),
            pltpu.SemaphoreType.DMA((2 * (rows // CHUNK) + 2,)),
        ],
        compiler_params=params(),
        name="states",
    )(*(in_hbm(x) for x in (lengths, key_rows, value_rows, decay_rows)))
    taken = lax.all_to_all(states, "seq", split_axis=0, concat_axis=0, tiled=True, axis_index_groups=chains)
    within, decayed, gain = pl.pallas_call(
        within_kernel,
        out_shape=(
            jax.ShapeDtypeStruct((rows, width), F32),
            jax.ShapeDtypeStruct((rows, width), BF16),
            jax.ShapeDtypeStruct((1, width), F32),
        ),
        in_specs=[smem, hbm, hbm, hbm, vmem, vmem],
        out_specs=(vmem, vmem, vmem),
        scratch_shapes=[pltpu.VMEM((rows, width), BF16)] * 3 + [pltpu.SemaphoreType.DMA((3,))],
        compiler_params=params(),
        cost_estimate=pl.CostEstimate(
            flops=4 * rows * rows * width, bytes_accessed=9 * rows * width, transcendentals=rows * rows * heads
        ),
        name="within",
    )(lengths, *(in_hbm(x) for x in (query_rows, key_rows, value_rows)), decay_rows, norm_gain.reshape(1, width))
    taken, within, decayed, gain = lax.optimization_barrier((taken, within, decayed, gain))
    total = pl.pallas_call(
        total_kernel,
        out_shape=jax.ShapeDtypeStruct((pairs, PAIR, dim), F32),
        in_specs=[vmem],
        out_specs=vmem,
        compiler_params=params(),
        name="total",
    )(taken)
    entering = lax.ppermute(total, "seq", onward)
    before, reach = pl.pallas_call(
        prefix_kernel,
        out_shape=(
            jax.ShapeDtypeStruct((holders, pairs, PAIR, dim), F32),
            jax.ShapeDtypeStruct((holders, PAIR, dim), F32),
        ),
        in_specs=[vmem],
        out_specs=(vmem, vmem),
        compiler_params=params(),
        cost_estimate=pl.CostEstimate(flops=2 * width * dim, bytes_accessed=6 * width * dim, transcendentals=holders),
        name="prefix",
    )(taken)
    given = pl.pallas_call(
        enter_kernel,
        out_shape=jax.ShapeDtypeStruct((holders, slots, dim), BF16),
        in_specs=[vmem] * 3,
        out_specs=vmem,
        compiler_params=params(),
        name="enter",
    )(before.reshape(width, dim), reach.reshape(holders * PAIR, dim), entering.reshape(slots, dim))
    incoming = lax.all_to_all(given, "seq", split_axis=0, concat_axis=0, tiled=True, axis_index_groups=chains)
    count = lax.axis_size("section")
    sections = list(ORDER_SECTION)
    normed = pl.pallas_call(
        functools.partial(finish_kernel, sections),
        out_shape=jax.ShapeDtypeStruct((count, rows // count, width), BF16),
        in_specs=[vmem] * 4,
        out_specs=vmem,
        compiler_params=params(),
        name="finish",
    )(within, decayed, incoming.reshape(width, dim), gain)
    landed = lax.all_to_all(
        normed, "section", split_axis=0, concat_axis=0, tiled=True, axis_index_groups=[sections]
    )
    return pl.pallas_call(
        functools.partial(place_kernel, sections),
        out_shape=jax.ShapeDtypeStruct((rows // count, count * width), BF16),
        in_specs=[vmem],
        out_specs=hbm,
        scratch_shapes=[pltpu.SemaphoreType.DMA((count,))],
        compiler_params=params(),
        name="place",
    )(landed)


def solution(mesh):
    placed = (
        P("seq", "section"),
        P("seq", "section"),
        P("seq", "section"),
        P("seq", "section"),
        P(),
        P("section"),
    )
    return jax.shard_map(
        shards, mesh=mesh, in_specs=placed, out_specs=P(("seq", "section"), None), check_vma=False
    )
```

```python
import functools
import math

import jax
import jax.numpy as jnp
from jax import lax
from jax.experimental import pallas as pl
from jax.experimental.pallas import tpu as pltpu
from jax.sharding import PartitionSpec as P

F32, BF16 = jnp.float32, jnp.bfloat16
NEVER = -1e30
PAIR = 2
CHUNK = 128
ORDER_Z = (8, 7, 6, 5, 4, 3, 2, 1, 0, 15, 14, 13, 12, 11, 10, 9)
ORDER_SECTION = (5, 4, 7, 6, 1, 0, 3, 2)


def in_chain(count):
    return sorted(range(count), key=lambda position: ORDER_Z[position])


def dot(a, b, contract):
    return lax.dot_general(a, b, ((contract[:1], contract[1:]), ((), ())), preferred_element_type=F32)


def three_parts(x):
    high = x.astype(BF16)
    rest = x - high.astype(F32)
    mid = rest.astype(BF16)
    return high, mid, (rest - mid.astype(F32)).astype(BF16)


def document_limits(lengths_ref, first_row, rows):
    last = first_row + rows - 1
    start_last, end_prev, begin = jnp.int32(0), jnp.int32(0), jnp.int32(0)
    found = jnp.bool_(False)
    for doc in range(lengths_ref.shape[0]):
        start_last = jnp.where(begin <= last, begin, start_last)
        end = begin + lengths_ref[doc]
        end_prev = jnp.where(found, end_prev, end)
        found = jnp.logical_or(found, end >= first_row)
        begin = end
    return start_last, end_prev


def state_kernel(lengths_hbm, key_hbm, value_hbm, decay_hbm, out_ref, lengths_ref, keys_ref, values_ref, decay_ref, sems):
    heads, rows = decay_ref.shape
    dim = keys_ref.shape[1] // heads
    holders, slots = out_ref.shape[0], heads * dim // out_ref.shape[0]
    chunks = rows // CHUNK
    small = [
        pltpu.make_async_copy(decay_hbm, decay_ref, sems.at[0]),
        pltpu.make_async_copy(lengths_hbm, lengths_ref, sems.at[1]),
    ]
    spans = [pl.ds(c * CHUNK, CHUNK) for c in range(chunks)]
    keys_in = [pltpu.make_async_copy(key_hbm.at[at], keys_ref.at[at], sems.at[2 + 2 * c]) for c, at in enumerate(spans)]
    values_in = [pltpu.make_async_copy(value_hbm.at[at], values_ref.at[at], sems.at[3 + 2 * c]) for c, at in enumerate(spans)]
    for copy in small:
        copy.start()
    for c in range(chunks):
        keys_in[c].start()
        values_in[c].start()
    row = lax.broadcasted_iota(jnp.int32, (CHUNK, CHUNK), 0)
    col = lax.broadcasted_iota(jnp.int32, (CHUNK, CHUNK), 1)
    later = (row > col).astype(F32).astype(BF16)
    small[0].wait()
    decay = jnp.concatenate([decay_ref[:, c * CHUNK : (c + 1) * CHUNK] for c in range(chunks)], axis=0)
    suffix = sum(dot(part, later, (1, 0)) for part in three_parts(decay))
    chunk_log = suffix[:, 0:1] + decay[:, 0:1]
    small[1].wait()
    first_row = lax.axis_index("seq") * rows
    start_last, _ = document_limits(lengths_ref, first_row, rows)
    scales = [None] * chunks
    end_log = jnp.zeros((heads, 1), F32)
    for c in reversed(range(chunks)):
        mine = slice(c * heads, (c + 1) * heads)
        position = first_row + c * CHUNK + lax.broadcasted_iota(jnp.int32, (1, CHUNK), 1)
        scales[c] = jnp.where(position >= start_last, jnp.exp(suffix[mine] + end_log), 0.0)
        end_log = end_log + chunk_log[mine]
    end_log = jnp.where(start_last >= first_row, NEVER, end_log)
    high, mid, low = (part.astype(F32) for part in three_parts(end_log))
    lane = lax.broadcasted_iota(jnp.int32, (PAIR, dim), 1)
    per_head = holders // heads
    scale = jnp.concatenate(scales, axis=1)
    for copy in keys_in + values_in:
        copy.wait()
    for head in range(heads):
        one = slice(head, head + 1)
        sent = jnp.where(lane == 0, high[one], jnp.where(lane == 1, mid[one], jnp.where(lane == 2, low[one], 0.0)))
        span = pl.ds(head * dim, dim)
        keys = (keys_ref[:, span].T.astype(F32) * scale[one, :]).astype(BF16)
        state = dot(keys, values_ref[:, span], (1, 0)).astype(BF16)
        for i in range(per_head):
            for pair in range(slots // PAIR):
                at = i * slots + pair * PAIR
                out_ref[head * per_head + i, pair] = state[at : at + PAIR, :]
            out_ref[head * per_head + i, slots // PAIR] = sent.astype(BF16)


def within_kernel(
    lengths_ref, query_hbm, key_hbm, value_hbm, decay_ref, gain_ref,
    within_ref, decayed_ref, staged_ref, query_ref, key_ref, value_ref, sems,
):
    heads, rows = decay_ref.shape
    fetched = [
        pltpu.make_async_copy(query_hbm, query_ref, sems.at[0]),
        pltpu.make_async_copy(key_hbm, key_ref, sems.at[1]),
        pltpu.make_async_copy(value_hbm, value_ref, sems.at[2]),
    ]
    for copy in fetched:
        copy.start()
    staged_ref[...] = gain_ref[...]
    dim = key_ref.shape[1] // heads
    scale = 1.0 / math.sqrt(dim)
    step = 128
    first_row = lax.axis_index("seq") * rows
    _, end_prev = document_limits(lengths_ref, first_row, rows)
    row = lax.broadcasted_iota(jnp.int32, (rows, rows), 0)
    col = lax.broadcasted_iota(jnp.int32, (rows, rows), 1)
    upto = (col <= row).astype(F32).astype(BF16)
    parts = three_parts(decay_ref[...])
    cumul_col = sum(dot(upto, part, (1, 1)) for part in parts)
    cumul_row = sum(dot(part, upto, (1, 1)) for part in parts)
    spot_row = first_row + lax.broadcasted_iota(jnp.int32, (1, rows), 1)
    lane = lax.broadcasted_iota(jnp.int32, (1, dim), 1)
    doc_row = jnp.zeros((1, rows), F32)
    ends = jnp.zeros((1, dim), jnp.int32)
    end = jnp.int32(0)
    for doc in range(lengths_ref.shape[0]):
        end = end + lengths_ref[doc]
        doc_row = doc_row + jnp.where(spot_row >= end, 1.0, 0.0)
        ends = ends + jnp.where(lane >= doc, lengths_ref[doc], 0)
    position = first_row + lax.broadcasted_iota(jnp.int32, (rows, 1), 0)
    doc_col = jnp.sum(jnp.where(ends <= position, 1.0, 0.0), axis=1, keepdims=True)
    for copy in fetched:
        copy.wait()
    query_scale = jnp.where(position < end_prev, jnp.exp(cumul_col) * scale, 0.0)
    for head in range(heads):
        span = pl.ds(head * dim, dim)
        decayed_ref[:, span] = (query_ref[:, span].astype(F32) * query_scale[:, head : head + 1]).astype(BF16)
    for at in range(0, rows, step):
        upper = at + step
        t = at + lax.broadcasted_iota(jnp.int32, (step, upper), 0)
        u = lax.broadcasted_iota(jnp.int32, (step, upper), 1)
        allowed = jnp.logical_and(u <= t, doc_col[at:upper] == doc_row[:, :upper])
        shut = jnp.where(allowed, 0.0, NEVER)
        for head in range(heads):
            span = pl.ds(head * dim, dim)
            scores = dot(query_ref[pl.ds(at, step), span], key_ref[pl.ds(0, upper), span], (1, 1))
            gap = cumul_col[at:upper, head : head + 1] - cumul_row[head : head + 1, :upper]
            weights = jnp.where(allowed, scores * scale * jnp.exp(jnp.minimum(gap, 0.0) + shut), 0.0).astype(BF16)
            within_ref[pl.ds(at, step), span] = dot(weights, value_ref[pl.ds(0, upper), span], (1, 0))


def kept_of(taken_ref, block):
    parts = taken_ref[block, taken_ref.shape[1] - 1].astype(F32)[0:1, 0:3]
    return jnp.exp(jnp.sum(parts, axis=1, keepdims=True))


def total_kernel(taken_ref, total_ref):
    blocks, pairs = taken_ref.shape[0], taken_ref.shape[1] - 1
    carry = jnp.zeros(total_ref.shape, F32)
    for block in in_chain(blocks):
        carry = taken_ref[block, 0:pairs].astype(F32) + kept_of(taken_ref, block) * carry
    total_ref[...] = carry.astype(BF16)


def prefix_kernel(taken_ref, before_ref, reach_ref):
    blocks, pairs = taken_ref.shape[0], taken_ref.shape[1] - 1
    carry = jnp.zeros(before_ref.shape[1:], F32)
    reach = jnp.ones((1, 1), F32)
    for block in in_chain(blocks):
        before_ref[block] = carry
        reach_ref[block] = jnp.broadcast_to(reach, reach_ref.shape[1:])
        kept = kept_of(taken_ref, block)
        carry = taken_ref[block, 0:pairs].astype(F32) + kept * carry
        reach = kept * reach


def enter_kernel(before_ref, reach_ref, entering_ref, out_ref):
    slots = entering_ref.shape[0]
    entering = entering_ref[...].astype(F32)
    for block in range(out_ref.shape[0]):
        at = pl.ds(block * slots, slots)
        reach = reach_ref[block * PAIR : block * PAIR + 1, :]
        out_ref[block] = (before_ref[at, :] + reach * entering).astype(BF16)


def finish_kernel(sections, within_ref, decayed_ref, incoming_ref, gain_ref, out_ref):
    dim = incoming_ref.shape[1]
    tokens = out_ref.shape[1]
    for head in range(incoming_ref.shape[0] // dim):
        span = pl.ds(head * dim, dim)
        carried = dot(decayed_ref[:, span], incoming_ref[span, :], (1, 0))
        attention = within_ref[:, span] + carried
        mean_square = jnp.mean(attention * attention, axis=1, keepdims=True)
        normed = (attention * lax.rsqrt(mean_square + 1e-05) * gain_ref[:, span]).astype(BF16)
        for i, section in enumerate(sections):
            out_ref[i, :, span] = normed[section * tokens : (section + 1) * tokens, :]


def place_kernel(sections, landed_ref, out_hbm, sems):
    width = landed_ref.shape[2]
    copies = [
        pltpu.make_async_copy(landed_ref.at[i], out_hbm.at[:, pl.ds(section * width, width)], sems.at[i])
        for i, section in enumerate(sections)
    ]
    for copy in copies:
        copy.start()
    for copy in copies:
        copy.wait()


def params():
    return pltpu.CompilerParams(vmem_limit_bytes=32 << 20)


def in_hbm(x):
    return pltpu.with_memory_space_constraint(x, pltpu.HBM)


def shards(query_rows, key_rows, value_rows, log_decay, lengths, norm_gain):
    rows, width = query_rows.shape
    heads = log_decay.shape[1]
    dim = width // heads
    holders = lax.axis_size("seq") // 4
    chains = [[at + z for z in ORDER_Z] for at in range(0, 4 * holders, holders)]
    onward = [(holders + i, 2 * holders + i) for i in range(holders)]
    slots = width // holders
    pairs = slots // PAIR
    decay_rows = log_decay.T
    hbm = pl.BlockSpec(memory_space=pltpu.HBM)
    smem = pl.BlockSpec(memory_space=pltpu.SMEM)
    vmem = pl.BlockSpec(memory_space=pltpu.VMEM)

    states = pl.pallas_call(
        state_kernel,
        out_shape=jax.ShapeDtypeStruct((holders, pairs + 1, PAIR, dim), BF16),
        in_specs=[hbm, hbm, hbm, hbm],
        out_specs=vmem,
        scratch_shapes=[
            pltpu.SMEM(lengths.shape, lengths.dtype),
            pltpu.VMEM((rows, width), BF16),
            pltpu.VMEM((rows, width), BF16),
            pltpu.VMEM((heads, rows), F32),
            pltpu.SemaphoreType.DMA((2 * (rows // CHUNK) + 2,)),
        ],
        compiler_params=params(),
        name="states",
    )(*(in_hbm(x) for x in (lengths, key_rows, value_rows, decay_rows)))
    taken = lax.all_to_all(states, "seq", split_axis=0, concat_axis=0, tiled=True, axis_index_groups=chains)
    within, decayed, gain = pl.pallas_call(
        within_kernel,
        out_shape=(
            jax.ShapeDtypeStruct((rows, width), F32),
            jax.ShapeDtypeStruct((rows, width), BF16),
            jax.ShapeDtypeStruct((1, width), F32),
        ),
        in_specs=[smem, hbm, hbm, hbm, vmem, vmem],
        out_specs=(vmem, vmem, vmem),
        scratch_shapes=[pltpu.VMEM((rows, width), BF16)] * 3 + [pltpu.SemaphoreType.DMA((3,))],
        compiler_params=params(),
        cost_estimate=pl.CostEstimate(
            flops=4 * rows * rows * width, bytes_accessed=9 * rows * width, transcendentals=rows * rows * heads
        ),
        name="within",
    )(lengths, *(in_hbm(x) for x in (query_rows, key_rows, value_rows)), decay_rows, norm_gain.reshape(1, width))
    taken, within, decayed, gain = lax.optimization_barrier((taken, within, decayed, gain))
    total = pl.pallas_call(
        total_kernel,
        out_shape=jax.ShapeDtypeStruct((pairs, PAIR, dim), BF16),
        in_specs=[vmem],
        out_specs=vmem,
        compiler_params=params(),
        name="total",
    )(taken)
    entering = lax.ppermute(total, "seq", onward)
    before, reach = pl.pallas_call(
        prefix_kernel,
        out_shape=(
            jax.ShapeDtypeStruct((holders, pairs, PAIR, dim), F32),
            jax.ShapeDtypeStruct((holders, PAIR, dim), F32),
        ),
        in_specs=[vmem],
        out_specs=(vmem, vmem),
        compiler_params=params(),
        cost_estimate=pl.CostEstimate(flops=2 * width * dim, bytes_accessed=6 * width * dim, transcendentals=holders),
        name="prefix",
    )(taken)
    given = pl.pallas_call(
        enter_kernel,
        out_shape=jax.ShapeDtypeStruct((holders, slots, dim), BF16),
        in_specs=[vmem] * 3,
        out_specs=vmem,
        compiler_params=params(),
        name="enter",
    )(before.reshape(width, dim), reach.reshape(holders * PAIR, dim), entering.reshape(slots, dim))
    incoming = lax.all_to_all(given, "seq", split_axis=0, concat_axis=0, tiled=True, axis_index_groups=chains)
    count = lax.axis_size("section")
    sections = list(ORDER_SECTION)
    normed = pl.pallas_call(
        functools.partial(finish_kernel, sections),
        out_shape=jax.ShapeDtypeStruct((count, rows // count, width), BF16),
        in_specs=[vmem] * 4,
        out_specs=vmem,
        compiler_params=params(),
        name="finish",
    )(within, decayed, incoming.reshape(width, dim), gain)
    landed = lax.all_to_all(
        normed, "section", split_axis=0, concat_axis=0, tiled=True, axis_index_groups=[sections]
    )
    return pl.pallas_call(
        functools.partial(place_kernel, sections),
        out_shape=jax.ShapeDtypeStruct((rows // count, count * width), BF16),
        in_specs=[vmem],
        out_specs=hbm,
        scratch_shapes=[pltpu.SemaphoreType.DMA((count,))],
        compiler_params=params(),
        name="place",
    )(landed)


def solution(mesh):
    placed = (
        P("seq", "section"),
        P("seq", "section"),
        P("seq", "section"),
        P("seq", "section"),
        P(),
        P("section"),
    )
    return jax.shard_map(
        shards, mesh=mesh, in_specs=placed, out_specs=P(("seq", "section"), None), check_vma=False
    )
```
